512 devices in a mesh: bin: 64 (over z, x, y_hi), grp: 8 (over y_lo, core).
Axes of the slice: x: 4, y: 8 (y_hi: 2, y_lo: 4; y = y_hi * 4 + y_lo), z: 8, core: 2. Of those that a mesh axis runs over, the one named last changes fastest.
Arguments:
- record: bfloat16 [8, 256, 8704], P('grp', 'bin'), may hold values from -60 to 60
- ref_index: int32 [8, 16], P('grp'), may hold values from 0 to 255, as said below
- offsets: int32 [16], replicated, may hold values from 0 to 7680, as said below
Outputs:
- transfer: bfloat16 [512, 2048, 256], P('bin', 'grp')
The draws below stay inside these ranges and needn't reach their ends.
Inputs may be any that keep to these rules, and one draw needn't show every extreme that they name: `ref_index`: each row lists 16 different channels of its group; every row holds 0 and 255. `offsets`: starts rise; the first is 0, the last is 7680, and neighbours lie 512 // 2 to 768 apart.
All inputs are finite; a program needn't handle non-finite values.
Results may differ from the reference program's by a relative error of at most 0.0095.
Values may be sent and summed in bfloat16 or wider, within the bound.
A program may use at most 64 MiB of HBM per device.

```python
import math
import jax
import jax.numpy as jnp
from jax import lax

C = 2048
R = 128
L = 1024
NB = 512
SEGS = 16
HOP = 512
NSAMP = 8704
GRP_COUNT = 8
CH_GRP = 256
REF_GRP = 16


def draw_record(key, part):
    key_noise, key_scale = jax.random.split(key, 2)
    shape_full = (GRP_COUNT, CH_GRP, NSAMP)
    chan_scale = jnp.exp(jax.random.uniform(key_scale, (GRP_COUNT, CH_GRP, 1), jnp.float32, 0.0, math.log(10.0)))
    noise = jnp.clip(jax.random.normal(key_noise, shape_full, jnp.float32), -6.0, 6.0)
    values = noise * chan_scale
    return values.astype(jnp.bfloat16)


def draw_ref_index(key, part):

    def one_group(group_key):
        key_pick, key_order = jax.random.split(group_key)
        middle = jax.random.permutation(key_pick, CH_GRP - 2)[:REF_GRP - 2].astype(jnp.int32) + 1
        chosen = jnp.concatenate([jnp.array([0, CH_GRP - 1], dtype=jnp.int32), middle])
        return jax.random.permutation(key_order, chosen)
    return jax.vmap(one_group)(jax.random.split(key, GRP_COUNT)).astype(jnp.int32)


def draw_offsets(key, part):
    jitter = jax.random.randint(key, (SEGS,), -(HOP // 4), HOP // 4 + 1, dtype=jnp.int32)
    segment_num = jnp.arange(SEGS, dtype=jnp.int32)
    inner = (segment_num > 0) & (segment_num < SEGS - 1)
    return (segment_num * HOP + jnp.where(inner, jitter, 0)).astype(jnp.int32)


def setup_inputs(seed: int = 0) -> dict:
    streams_of = jax.random.split(jax.random.key(seed), 4)
    return {
        "record": draw_record(jax.random.fold_in(streams_of[3], 71), 0),
        "ref_index": draw_ref_index(jax.random.fold_in(streams_of[3], 71), 0),
        "offsets": draw_offsets(jax.random.fold_in(streams_of[3], 71), 0),
    }


ridge_weight = 0.5

def make_table(seg_len, bins):
    sample_num = lax.iota(jnp.int32, seg_len)[:, None]
    bin_num = lax.iota(jnp.int32, bins)[None, :]
    angles = (sample_num * bin_num % seg_len).astype(jnp.float32) * (2.0 * math.pi / seg_len)
    hann_window = 0.5 - 0.5 * jnp.cos(sample_num.astype(jnp.float32) * (2.0 * math.pi / seg_len))
    return jnp.concatenate([hann_window * jnp.cos(angles), -(hann_window * jnp.sin(angles))], axis=1).astype(jnp.bfloat16)

def reference(record, ref_index, offsets):
    chan_rows = record.reshape(C, NSAMP)
    dft_table = make_table(L, NB).astype(jnp.float32)

    def one_segment(start_at):
        piece = lax.dynamic_slice_in_dim(chan_rows, start_at, L, 1).astype(jnp.float32)
        return jnp.dot(piece.astype(jnp.float32), dft_table.astype(jnp.float32), precision=lax.Precision.HIGHEST, preferred_element_type=jnp.float32).astype(jnp.bfloat16)
    spectra = lax.map(one_segment, offsets)
    spectra = jnp.transpose(spectra.reshape(SEGS, C, 2, NB), (3, 2, 0, 1))
    ref_channel = (ref_index + jnp.arange(GRP_COUNT, dtype=jnp.int32)[:, None] * CH_GRP).reshape(R).astype(jnp.int32)

    def one_bin(chan_spec):
        refs = jnp.take(chan_spec, ref_channel, axis=2).astype(jnp.float32)
        ref_real = refs[0]
        ref_imag = refs[1]
        ref_blocks = jnp.stack([jnp.concatenate([ref_real, -ref_imag], axis=-1), jnp.concatenate([ref_imag, ref_real], axis=-1)]).reshape(2 * SEGS, 2 * R)
        gram_small = jnp.dot(ref_blocks.astype(jnp.float32), ref_blocks.T.astype(jnp.float32), precision=lax.Precision.HIGHEST, preferred_element_type=jnp.float32)
        ridge_term = ridge_weight * jnp.trace(gram_small) / (2 * R)
        factor = jnp.linalg.cholesky(gram_small + ridge_term * jnp.eye(2 * SEGS, dtype=jnp.float32))
        chan_cols = chan_spec.reshape(2 * SEGS, C).astype(jnp.float32)
        solved = jax.scipy.linalg.cho_solve((factor, True), chan_cols)
        transfer_t = jnp.dot(ref_blocks.T.astype(jnp.float32), solved.astype(jnp.float32), precision=lax.Precision.HIGHEST, preferred_element_type=jnp.float32)
        return transfer_t.T.astype(jnp.bfloat16)
    return lax.map(one_bin, spectra)
```

```python
import math

import jax
import jax.numpy as jnp
import ml_dtypes
import numpy as np
from jax import lax
from jax.experimental import pallas as pl
from jax.experimental.pallas import tpu as pltpu
from jax.sharding import PartitionSpec as P

L = 1024
NB = 512
SEGS = 16
CH = 4
BINS = 8
REFS = 16
LANES = 128
TILES = 8704 // LANES
WINDOW = L + LANES
RIDGE = 0.5

F32 = jnp.float32
BF16 = jnp.bfloat16
MESH = pl.DeviceIdType.MESH


def make_table(bin_devices):
    n = np.arange(L)
    angles = (n[:, None] * np.arange(NB)[None, :] % L).astype(np.float32)
    angles = angles * np.float32(2.0 * math.pi / L)
    hann = np.float32(0.5) - np.float32(0.5) * np.cos(
        n.astype(np.float32) * np.float32(2.0 * math.pi / L)
    )
    parts = np.stack([hann[:, None] * np.cos(angles), -(hann[:, None] * np.sin(angles))])
    parts = parts.reshape(2, L, bin_devices, 2, 4)
    return parts.transpose(4, 0, 2, 3, 1).reshape(2 * NB, L).astype(ml_dtypes.bfloat16)


def nt_dot(a, b):
    return lax.dot_general(a, b, (((1,), (1,)), ((), ())), preferred_element_type=F32)


def tn_dot(a, b):
    return lax.dot_general(a, b, (((0,), (0,)), ((), ())), preferred_element_type=F32)


def cut_segments(offsets, record, segs):
    for s in range(SEGS):
        tile = jnp.minimum(lax.div(offsets[s], LANES), TILES - WINDOW // LANES)
        start = pl.multiple_of(tile * LANES, LANES)
        window = record[0, :, pl.ds(start, WINDOW)].astype(F32)
        window = jnp.concatenate([window, window], axis=0)
        back = lax.rem(WINDOW - (offsets[s] - start), WINDOW)
        cut = pltpu.roll(window, back, axis=1)
        for t in range(L // LANES):
            segs[t, pl.ds(s, CH, stride=SEGS), :] = cut[:CH, t * LANES : (t + 1) * LANES]


def pack_spectra(segs, table, stage, send):
    rows = jnp.concatenate([segs[t] for t in range(L // LANES)], axis=1).astype(BF16)
    rows = jnp.concatenate([rows, rows], axis=0)
    blocks = [nt_dot(table[pl.ds(g * LANES, LANES), :], rows) for g in range(8)]
    group = lax.broadcasted_iota(jnp.int32, (LANES, LANES), 1) // SEGS
    turned = []
    for r in range(4):
        mixed = blocks[r]
        for q in range(1, 8):
            mixed = jnp.where(group == q, blocks[(q + r) % 8], mixed)
        turned.append(pltpu.roll(mixed, SEGS * r, axis=1) if r else mixed)
    phase = lax.rem(group, 4)
    for c in range(CH):
        out = turned[(0 - c) % 4]
        for g in range(1, 4):
            out = jnp.where(phase == g, turned[(g - c) % 4], out)
        stage[pl.ds(c, LANES, stride=CH), :] = out
    send[...] = stage[...].reshape(send.shape).astype(BF16)


def pick_references(ref_index, recv):
    shape = (2 * REFS, recv.shape[0] * BINS)
    row = lax.broadcasted_iota(jnp.int32, shape, 0)
    col = lax.broadcasted_iota(jnp.int32, shape, 1)
    wanted = jnp.full((2 * REFS, 1), -1, jnp.int32)
    slot = lax.broadcasted_iota(jnp.int32, (2 * REFS, 1), 0)
    for i in range(REFS):
        wanted = jnp.where(lax.rem(slot, REFS) == i, ref_index[0, i], wanted)
    place = (wanted // CH) * BINS + lax.rem(wanted, CH) + (row // REFS) * CH
    chosen = jnp.where(col == place, 1.0, 0.0).astype(BF16)
    rows = recv[...].astype(F32).reshape(shape[1], LANES).astype(BF16)
    return jnp.dot(chosen, rows, preferred_element_type=F32).astype(BF16)


def cut_kernel(offsets_hbm, record_hbm, segs, offsets, record, sems):
    load_offsets = pltpu.make_async_copy(offsets_hbm, offsets, sems.at[0])
    load_record = pltpu.make_async_copy(record_hbm, record, sems.at[1])
    load_offsets.start()
    load_record.start()
    load_offsets.wait()
    load_record.wait()
    cut_segments(offsets, record, segs)


def exchange_kernel(ref_index_hbm, segs, table, recv, refs, ref_index, stage, send, sems):
    bins, grps = lax.axis_size("bin"), lax.axis_size("grp")
    me, grp = lax.axis_index("bin"), lax.axis_index("grp")
    load = pltpu.make_async_copy(ref_index_hbm, ref_index, sems.at[0])
    load.start()
    barrier = pltpu.get_barrier_semaphore()

    @pl.loop(1, bins)
    def _(k):
        peer = lax.rem(me + k, bins)
        pl.semaphore_signal(barrier, 1, device_id={"bin": peer}, device_id_type=MESH)

    @pl.loop(1, grps)
    def _(k):
        peer = lax.rem(grp + k, grps)
        pl.semaphore_signal(barrier, 1, device_id={"grp": peer}, device_id_type=MESH)

    pack_spectra(segs, table, stage, send)
    pl.semaphore_wait(barrier, bins + grps - 2)

    @pl.loop(1, bins)
    def _(k):
        peer = lax.rem(me + k, bins)
        pltpu.make_async_remote_copy(
            src_ref=send.at[peer],
            dst_ref=recv.at[me],
            send_sem=sems.at[1],
            recv_sem=sems.at[2],
            device_id={"bin": peer},
            device_id_type=MESH,
        ).start()

    recv[pl.ds(me, 1)] = send[pl.ds(me, 1)]
    load.wait()
    others = recv.at[pl.ds(0, bins - 1)]
    pltpu.make_async_copy(others, others, sems.at[2]).wait()
    refs[pl.ds(grp, 1)] = pick_references(ref_index, recv).reshape(1, 2, REFS, LANES)

    @pl.loop(1, grps)
    def _(k):
        peer = lax.rem(grp + k, grps)
        pltpu.make_async_remote_copy(
            src_ref=refs.at[grp],
            dst_ref=refs.at[grp],
            send_sem=sems.at[3],
            recv_sem=sems.at[4],
            device_id={"grp": peer},
            device_id_type=MESH,
        ).start()

    sent = send.at[pl.ds(0, bins - 1)]
    pltpu.make_async_copy(sent, sent, sems.at[1]).wait()
    other_refs = refs.at[pl.ds(0, grps - 1)]
    pltpu.make_async_copy(other_refs, other_refs, sems.at[4]).wait()
    pltpu.make_async_copy(other_refs, other_refs, sems.at[3]).wait()


def turn(x, imag):
    back = pltpu.roll(x, LANES - SEGS, axis=1)
    ahead = pltpu.roll(x, SEGS, axis=1)
    return jnp.where(imag, ahead, -back)


def lane_pick(x, index):
    return jnp.take_along_axis(x, index, axis=1, mode="promise_in_bounds")


def invert(z, lane, row):
    imag = lax.rem(lane, 32) >= SEGS
    inner = lax.rem(lane, 32)
    base = lane - inner
    segment = lax.rem(row, SEGS)
    for k in range(SEGS):
        col_re = lane_pick(z, base + k)
        col_im = lane_pick(z, base + (SEGS + k))
        pivot_row = jnp.concatenate(
            [
                jnp.broadcast_to(z[h * SEGS + k : h * SEGS + k + 1], (SEGS, LANES))
                for h in range(2)
            ],
            axis=0,
        )
        pivot = jnp.concatenate(
            [
                jnp.broadcast_to(col_re[h * SEGS + k : h * SEGS + k + 1], (SEGS, LANES))
                for h in range(2)
            ],
            axis=0,
        )
        inverse = 1.0 / pivot
        in_col = lax.rem(lane, SEGS) == k
        unit = jnp.where(inner == k, 1.0, 0.0)
        pivot_row = jnp.where(in_col, unit, pivot_row)
        scaled = pivot_row * inverse
        turned = turn(scaled, imag)
        is_row = segment == k
        col_re = jnp.where(is_row, -1.0, col_re)
        col_im = jnp.where(is_row, 0.0, col_im)
        rest = jnp.where(is_row | in_col, 0.0, z)
        z = rest - col_re * scaled - col_im * turned
    return z


def split(x):
    hi = x.astype(BF16)
    return hi, (x - hi.astype(F32)).astype(BF16)


def solve_kernel(recv, refs, out, flat, chans, result, sems):
    sources = recv.shape[0]
    ranks = refs.shape[0] * REFS
    flat[...] = recv[...].astype(F32).reshape(flat.shape)
    for h in range(2):
        for c in range(CH):
            chans[h, pl.ds(c, sources, stride=CH), :] = flat[
                pl.ds(h * CH + c, sources, stride=BINS), :
            ]

    lane = lax.broadcasted_iota(jnp.int32, (LANES, LANES), 1)
    row = lax.broadcasted_iota(jnp.int32, (LANES, LANES), 0)
    same = (lane // 32) == (row // 32)
    lane32, row32 = lane[:32], row[:32]
    inner32 = lax.rem(lane32, 32)
    blocks, grams, ridges = [], [], []
    for h in range(2):
        x = refs[:, h].reshape(ranks, LANES).astype(F32)
        imag = lax.rem(lax.broadcasted_iota(jnp.int32, x.shape, 1), 32) >= SEGS
        block = jnp.concatenate([x, turn(x, imag)], axis=0).astype(BF16)
        blocks.append(block)
        gram = jnp.where(same, tn_dot(block, block), 0.0)
        gram = gram[0:32] + gram[32:64] + gram[64:96] + gram[96:128]
        diagonal = jnp.where(inner32 == row32, gram, 0.0)
        diagonal = jnp.sum(diagonal, axis=0, keepdims=True)
        group_ones = jnp.where(same, 1.0, 0.0)
        trace = jnp.dot(
            jnp.broadcast_to(diagonal, (8, LANES)),
            group_ones,
            precision=lax.Precision.HIGHEST,
            preferred_element_type=F32,
        )
        ridge = (RIDGE / (2 * ranks)) * trace[:1]
        grams.append(gram[:SEGS] + jnp.where(inner32[:SEGS] == row32[:SEGS], ridge, 0.0))

    inverses = invert(jnp.concatenate(grams, axis=0), lane32, row32)
    imag16 = lax.rem(lane[:SEGS], 32) >= SEGS
    copies = []
    for h in range(2):
        upper = inverses[h * SEGS : (h + 1) * SEGS]
        full = jnp.concatenate([upper, turn(upper, imag16)], axis=0)
        full = jnp.where(same, jnp.concatenate([full] * 4, axis=0), 0.0)
        hi, lo = split(full)
        solved = nt_dot(hi, blocks[h]) + nt_dot(lo, blocks[h])
        y = chans[h].astype(BF16)
        y = jnp.concatenate([y, y], axis=1)
        owner = lax.broadcasted_iota(jnp.int32, solved.shape, 0) // 32
        for b in range(4):
            hi, lo = split(jnp.where(owner == b, solved, 0.0))
            weights = jnp.concatenate([hi, lo], axis=0)
            f = h * 4 + b
            result[f] = jnp.dot(y, weights, preferred_element_type=F32).astype(BF16)
            copy = pltpu.make_async_copy(result.at[f], out.at[f], sems.at[f])
            copy.start()
            copies.append(copy)
    for copy in copies:
        copy.wait()


def cut(record, offsets):
    hbm = pl.BlockSpec(memory_space=pltpu.HBM)
    return pl.pallas_call(
        cut_kernel,
        out_shape=jax.ShapeDtypeStruct((L // LANES, CH * SEGS, LANES), F32),
        in_specs=[hbm, hbm],
        out_specs=pl.BlockSpec(memory_space=pltpu.VMEM),
        scratch_shapes=[
            pltpu.SMEM(offsets.shape, jnp.int32),
            pltpu.VMEM(record.shape, BF16),
            pltpu.SemaphoreType.DMA((2,)),
        ],
        compiler_params=pltpu.CompilerParams(vmem_limit_bytes=16 << 20),
        cost_estimate=pl.CostEstimate(flops=0, transcendentals=0, bytes_accessed=6 << 20),
    )(offsets, record)


def exchange(segs, ref_index, table):
    bins, grps = lax.axis_size("bin"), lax.axis_size("grp")
    vmem = pl.BlockSpec(memory_space=pltpu.VMEM)
    return pl.pallas_call(
        exchange_kernel,
        out_shape=(
            jax.ShapeDtypeStruct((bins, BINS, LANES), BF16),
            jax.ShapeDtypeStruct((grps, 2, REFS, LANES), BF16),
        ),
        in_specs=[pl.BlockSpec(memory_space=pltpu.HBM), vmem, vmem],
        out_specs=(vmem, vmem),
        scratch_shapes=[
            pltpu.SMEM(ref_index.shape, jnp.int32),
            pltpu.VMEM((2 * CH * bins, LANES), F32),
            pltpu.VMEM((bins, BINS, LANES), BF16),
            pltpu.SemaphoreType.DMA((5,)),
        ],
        compiler_params=pltpu.CompilerParams(
            collective_id=0, has_side_effects=True, vmem_limit_bytes=16 << 20
        ),
    )(ref_index, segs, table)


def solve(recv, refs):
    sources = recv.shape[0]
    chans = sources * CH
    vmem = pl.BlockSpec(memory_space=pltpu.VMEM)
    width = 2 * refs.shape[0] * REFS
    return pl.pallas_call(
        solve_kernel,
        out_shape=jax.ShapeDtypeStruct((BINS, chans, width), BF16),
        in_specs=[vmem, vmem],
        out_specs=pl.BlockSpec(memory_space=pl.ANY),
        scratch_shapes=[
            pltpu.VMEM((sources * BINS, LANES), F32),
            pltpu.VMEM((2, chans, LANES), F32),
            pltpu.VMEM((BINS, chans, width), BF16),
            pltpu.SemaphoreType.DMA((BINS,)),
        ],
        compiler_params=pltpu.CompilerParams(vmem_limit_bytes=16 << 20),
    )(recv, refs)


def local(record, ref_index, offsets):
    table = jnp.asarray(make_table(lax.axis_size("bin")))
    recv, refs = exchange(cut(record, offsets), ref_index, table)
    return solve(recv, refs)


def solution(mesh):
    placed = (P("grp", "bin", None), P("grp", None), P())
    return jax.shard_map(
        local, mesh=mesh, in_specs=placed, out_specs=P("bin", "grp", None), check_vma=False
    )
```

```python
import math

import jax
import jax.numpy as jnp
import ml_dtypes
import numpy as np
from jax import lax
from jax.experimental import pallas as pl
from jax.experimental.pallas import tpu as pltpu
from jax.sharding import PartitionSpec as P

L = 1024
NB = 512
SEGS = 16
CH = 4
BINS = 8
REFS = 16
LANES = 128
TILES = 8704 // LANES
WINDOW = L + LANES
RIDGE = 0.5
VMEM_LIMIT = 16 << 20

F32 = jnp.float32
BF16 = jnp.bfloat16
MESH = pl.DeviceIdType.MESH


def make_table(bin_devices):
    n = np.arange(L)
    angles = (n[:, None] * np.arange(NB)[None, :] % L).astype(np.float32)
    angles = angles * np.float32(2.0 * math.pi / L)
    hann = np.float32(0.5) - np.float32(0.5) * np.cos(
        n.astype(np.float32) * np.float32(2.0 * math.pi / L)
    )
    parts = np.stack([hann[:, None] * np.cos(angles), -(hann[:, None] * np.sin(angles))])
    parts = parts.reshape(2, L, bin_devices, 2, 4)
    return parts.transpose(4, 0, 2, 3, 1).reshape(8, LANES, L).astype(ml_dtypes.bfloat16)


def nt_dot(a, b):
    return lax.dot_general(a, b, (((1,), (1,)), ((), ())), preferred_element_type=F32)


def tn_dot(a, b):
    return lax.dot_general(a, b, (((0,), (0,)), ((), ())), preferred_element_type=F32)


def cut_segments(offsets, record, segs):
    for s in range(SEGS):
        tile = jnp.minimum(lax.div(offsets[s], LANES), TILES - WINDOW // LANES)
        start = pl.multiple_of(tile * LANES, LANES)
        window = record[0, :, pl.ds(start, WINDOW)].astype(F32)
        window = jnp.concatenate([window, window], axis=0)
        back = lax.rem(WINDOW - (offsets[s] - start), WINDOW)
        cut = pltpu.roll(window, back, axis=1)
        for t in range(L // LANES):
            segs[t, pl.ds(s, CH, stride=SEGS), :] = cut[:CH, t * LANES : (t + 1) * LANES]


def pack_spectra(segs, table, loads, stage, send):
    rows = jnp.concatenate([segs[t] for t in range(L // LANES)], axis=1).astype(BF16)
    rows = jnp.concatenate([rows, rows], axis=0)
    blocks = []
    for g in range(8):
        loads[g].wait()
        blocks.append(nt_dot(table[g], rows))
    group = lax.broadcasted_iota(jnp.int32, (LANES, LANES), 1) // SEGS
    turned = []
    for r in range(4):
        mixed = blocks[r]
        for q in range(1, 8):
            mixed = jnp.where(group == q, blocks[(q + r) % 8], mixed)
        turned.append(pltpu.roll(mixed, SEGS * r, axis=1) if r else mixed)
    phase = lax.rem(group, 4)
    for c in range(CH):
        out = turned[(0 - c) % 4]
        for g in range(1, 4):
            out = jnp.where(phase == g, turned[(g - c) % 4], out)
        stage[pl.ds(c, LANES, stride=CH), :] = out
    send[...] = stage[...].reshape(send.shape).astype(BF16)


def pick_references(ref_index, recv):
    shape = (2 * REFS, recv.shape[0] * BINS)
    row = lax.broadcasted_iota(jnp.int32, shape, 0)
    col = lax.broadcasted_iota(jnp.int32, shape, 1)
    wanted = jnp.full((2 * REFS, 1), -1, jnp.int32)
    slot = lax.broadcasted_iota(jnp.int32, (2 * REFS, 1), 0)
    for i in range(REFS):
        wanted = jnp.where(lax.rem(slot, REFS) == i, ref_index[0, i], wanted)
    place = (wanted // CH) * BINS + lax.rem(wanted, CH) + (row // REFS) * CH
    chosen = jnp.where(col == place, 1.0, 0.0).astype(BF16)
    rows = recv[...].astype(F32).reshape(shape[1], LANES).astype(BF16)
    return jnp.dot(chosen, rows, preferred_element_type=F32).astype(BF16)


def spectra_kernel(
    offsets_hbm, record_hbm, table_hbm, send, offsets, record, table, segs, stage, sems, table_sems
):
    load_offsets = pltpu.make_async_copy(offsets_hbm, offsets, sems.at[0])
    load_record = pltpu.make_async_copy(record_hbm, record, sems.at[1])
    loads = [
        pltpu.make_async_copy(table_hbm.at[g], table.at[g], table_sems.at[g]) for g in range(8)
    ]
    for load in (load_record, load_offsets, *loads):
        load.start()
    load_offsets.wait()
    load_record.wait()
    cut_segments(offsets, record, segs)
    pack_spectra(segs, table, loads, stage, send)


def exchange_kernel(ref_index_hbm, send, recv, refs, ref_index, sems, bin_in, grp_in):
    bins, grps = lax.axis_size("bin"), lax.axis_size("grp")
    me, grp = lax.axis_index("bin"), lax.axis_index("grp")
    load_refs = pltpu.make_async_copy(ref_index_hbm, ref_index, sems.at[0])
    load_refs.start()

    barrier = pltpu.get_barrier_semaphore()

    @pl.loop(me + 1, bins)
    def _(peer):
        pl.semaphore_signal(barrier, 1, device_id={"bin": peer}, device_id_type=MESH)

    @pl.loop(grp + 1, grps)
    def _(peer):
        pl.semaphore_signal(barrier, 1, device_id={"grp": peer}, device_id_type=MESH)

    @pl.when(me + grp > 0)
    def _():
        pl.semaphore_wait(barrier, me + grp)

    def send_to(peer):
        pltpu.make_async_remote_copy(
            src_ref=send.at[peer],
            dst_ref=recv.at[me],
            send_sem=sems.at[1],
            recv_sem=sems.at[2],
            device_id={"bin": peer},
            device_id_type=MESH,
        ).start()

    @pl.loop(0, me)
    def _(peer):
        send_to(peer)

    @pl.loop(0, me)
    def _(peer):
        pl.semaphore_signal(
            bin_in.at[me], 1, device_id={"bin": peer}, device_id_type=MESH
        )

    @pl.loop(0, grp)
    def _(peer):
        pl.semaphore_signal(
            grp_in.at[grp], 1, device_id={"grp": peer}, device_id_type=MESH
        )

    recv[pl.ds(me, 1)] = send[pl.ds(me, 1)]

    @pl.loop(me + 1, bins)
    def _(peer):
        pl.semaphore_wait(bin_in.at[peer], 1)
        send_to(peer)

    @pl.loop(grp + 1, grps)
    def _(peer):
        pl.semaphore_wait(grp_in.at[peer], 1)

    load_refs.wait()
    others = recv.at[pl.ds(0, bins - 1)]
    pltpu.make_async_copy(others, others, sems.at[2]).wait()
    refs[pl.ds(grp, 1)] = pick_references(ref_index, recv).reshape(1, 2, REFS, LANES)

    @pl.loop(1, grps)
    def _(k):
        peer = lax.rem(grp + k, grps)
        pltpu.make_async_remote_copy(
            src_ref=refs.at[grp],
            dst_ref=refs.at[grp],
            send_sem=sems.at[3],
            recv_sem=sems.at[4],
            device_id={"grp": peer},
            device_id_type=MESH,
        ).start()

    sent = send.at[pl.ds(0, bins - 1)]
    pltpu.make_async_copy(sent, sent, sems.at[1]).wait()
    other_refs = refs.at[pl.ds(0, grps - 1)]
    pltpu.make_async_copy(other_refs, other_refs, sems.at[4]).wait()
    pltpu.make_async_copy(other_refs, other_refs, sems.at[3]).wait()


def turn(x, imag):
    back = pltpu.roll(x, LANES - SEGS, axis=1)
    ahead = pltpu.roll(x, SEGS, axis=1)
    return jnp.where(imag, ahead, -back)


def lane_pick(x, index):
    return jnp.take_along_axis(x, index, axis=1, mode="promise_in_bounds")


def invert(z, lane, row):
    imag = lax.rem(lane, 32) >= SEGS
    inner = lax.rem(lane, 32)
    base = lane - inner
    segment = lax.rem(row, SEGS)
    for k in range(SEGS):
        col_re = lane_pick(z, base + k)
        col_im = lane_pick(z, base + (SEGS + k))
        pivot_row = jnp.concatenate(
            [
                jnp.broadcast_to(z[h * SEGS + k : h * SEGS + k + 1], (SEGS, LANES))
                for h in range(2)
            ],
            axis=0,
        )
        pivot = jnp.concatenate(
            [
                jnp.broadcast_to(col_re[h * SEGS + k : h * SEGS + k + 1], (SEGS, LANES))
                for h in range(2)
            ],
            axis=0,
        )
        inverse = 1.0 / pivot
        in_col = lax.rem(lane, SEGS) == k
        unit = jnp.where(inner == k, 1.0, 0.0)
        pivot_row = jnp.where(in_col, unit, pivot_row)
        scaled = pivot_row * inverse
        turned = turn(scaled, imag)
        is_row = segment == k
        col_re = jnp.where(is_row, -1.0, col_re)
        col_im = jnp.where(is_row, 0.0, col_im)
        rest = jnp.where(is_row | in_col, 0.0, z)
        z = rest - col_re * scaled - col_im * turned
    return z


def split(x):
    hi = x.astype(BF16)
    return hi, (x - hi.astype(F32)).astype(BF16)


def solve_kernel(recv, refs, out, flat, chans, result, sems):
    sources = recv.shape[0]
    ranks = refs.shape[0] * REFS
    flat[...] = recv[...].astype(F32).reshape(flat.shape)
    for h in range(2):
        for c in range(CH):
            chans[h, pl.ds(c, sources, stride=CH), :] = flat[
                pl.ds(h * CH + c, sources, stride=BINS), :
            ]

    lane = lax.broadcasted_iota(jnp.int32, (LANES, LANES), 1)
    row = lax.broadcasted_iota(jnp.int32, (LANES, LANES), 0)
    same = (lane // 32) == (row // 32)
    lane32, row32 = lane[:32], row[:32]
    inner32 = lax.rem(lane32, 32)
    blocks, grams, ridges = [], [], []
    for h in range(2):
        x = refs[:, h].reshape(ranks, LANES).astype(F32)
        imag = lax.rem(lax.broadcasted_iota(jnp.int32, x.shape, 1), 32) >= SEGS
        block = jnp.concatenate([x, turn(x, imag)], axis=0).astype(BF16)
        blocks.append(block)
        gram = jnp.where(same, tn_dot(block, block), 0.0)
        gram = gram[0:32] + gram[32:64] + gram[64:96] + gram[96:128]
        diagonal = jnp.where(inner32 == row32, gram, 0.0)
        diagonal = jnp.sum(diagonal, axis=0, keepdims=True)
        group_ones = jnp.where(same, 1.0, 0.0)
        trace = jnp.dot(
            jnp.broadcast_to(diagonal, (8, LANES)),
            group_ones,
            precision=lax.Precision.HIGHEST,
            preferred_element_type=F32,
        )
        ridge = (RIDGE / (2 * ranks)) * trace[:1]
        grams.append(gram[:SEGS] + jnp.where(inner32[:SEGS] == row32[:SEGS], ridge, 0.0))

    inverses = invert(jnp.concatenate(grams, axis=0), lane32, row32)
    imag16 = lax.rem(lane[:SEGS], 32) >= SEGS
    copies = []
    for h in range(2):
        upper = inverses[h * SEGS : (h + 1) * SEGS]
        full = jnp.concatenate([upper, turn(upper, imag16)], axis=0)
        full = jnp.where(same, jnp.concatenate([full] * 4, axis=0), 0.0)
        hi, lo = split(full)
        solved = nt_dot(hi, blocks[h]) + nt_dot(lo, blocks[h])
        y = chans[h].astype(BF16)
        y = jnp.concatenate([y, y], axis=1)
        owner = lax.broadcasted_iota(jnp.int32, solved.shape, 0) // 32
        for b in range(4):
            hi, lo = split(jnp.where(owner == b, solved, 0.0))
            weights = jnp.concatenate([hi, lo], axis=0)
            f = h * 4 + b
            result[f] = jnp.dot(y, weights, preferred_element_type=F32).astype(BF16)
            copy = pltpu.make_async_copy(result.at[f], out.at[f], sems.at[f])
            copy.start()
            copies.append(copy)
    for copy in copies:
        copy.wait()


def in_hbm(x):
    return pltpu.with_memory_space_constraint(x, pltpu.HBM)


def spectra(record, offsets, table):
    hbm = pl.BlockSpec(memory_space=pltpu.HBM)
    bins = lax.axis_size("bin")
    return pl.pallas_call(
        spectra_kernel,
        out_shape=jax.ShapeDtypeStruct((bins, BINS, LANES), BF16),
        in_specs=[hbm, hbm, hbm],
        out_specs=pl.BlockSpec(memory_space=pltpu.VMEM),
        scratch_shapes=[
            pltpu.SMEM(offsets.shape, jnp.int32),
            pltpu.VMEM(record.shape, BF16),
            pltpu.VMEM(table.shape, BF16),
            pltpu.VMEM((L // LANES, CH * SEGS, LANES), F32),
            pltpu.VMEM((2 * CH * bins, LANES), F32),
            pltpu.SemaphoreType.DMA((2,)),
            pltpu.SemaphoreType.DMA((8,)),
        ],
        compiler_params=pltpu.CompilerParams(vmem_limit_bytes=VMEM_LIMIT),
    )(*(in_hbm(x) for x in (offsets, record, table)))


def exchange(send, ref_index):
    bins, grps = lax.axis_size("bin"), lax.axis_size("grp")
    vmem = pl.BlockSpec(memory_space=pltpu.VMEM)
    return pl.pallas_call(
        exchange_kernel,
        out_shape=(
            jax.ShapeDtypeStruct((bins, BINS, LANES), BF16),
            jax.ShapeDtypeStruct((grps, 2, REFS, LANES), BF16),
        ),
        in_specs=[pl.BlockSpec(memory_space=pltpu.HBM), vmem],
        out_specs=(vmem, vmem),
        scratch_shapes=[
            pltpu.SMEM(ref_index.shape, jnp.int32),
            pltpu.SemaphoreType.DMA((5,)),
            pltpu.SemaphoreType.REGULAR((bins,)),
            pltpu.SemaphoreType.REGULAR((grps,)),
        ],
        compiler_params=pltpu.CompilerParams(
            collective_id=0, has_side_effects=True, vmem_limit_bytes=VMEM_LIMIT
        ),
    )(in_hbm(ref_index), send)


def solve(recv, refs):
    sources = recv.shape[0]
    chans = sources * CH
    vmem = pl.BlockSpec(memory_space=pltpu.VMEM)
    width = 2 * refs.shape[0] * REFS
    return pl.pallas_call(
        solve_kernel,
        out_shape=jax.ShapeDtypeStruct((BINS, chans, width), BF16),
        in_specs=[vmem, vmem],
        out_specs=pl.BlockSpec(memory_space=pl.ANY),
        scratch_shapes=[
            pltpu.VMEM((sources * BINS, LANES), F32),
            pltpu.VMEM((2, chans, LANES), F32),
            pltpu.VMEM((BINS, chans, width), BF16),
            pltpu.SemaphoreType.DMA((BINS,)),
        ],
        compiler_params=pltpu.CompilerParams(vmem_limit_bytes=VMEM_LIMIT),
    )(recv, refs)


def local(record, ref_index, offsets):
    table = jnp.asarray(make_table(lax.axis_size("bin")))
    recv, refs = exchange(spectra(record, offsets, table), ref_index)
    return solve(recv, refs)


def solution(mesh):
    placed = (P("grp", "bin", None), P("grp", None), P())
    return jax.shard_map(
        local, mesh=mesh, in_specs=placed, out_specs=P("bin", "grp", None), check_vma=False
    )
```

```python
import math

import jax
import jax.numpy as jnp
import ml_dtypes
import numpy as np
from jax import lax
from jax.experimental import pallas as pl
from jax.experimental.pallas import tpu as pltpu
from jax.sharding import PartitionSpec as P

L = 1024
NB = 512
SEGS = 16
CH = 4
BINS = 8
REFS = 16
LANES = 128
TILES = 8704 // LANES
STEPS = L // LANES + 1
RIDGE = 0.5
VMEM_LIMIT = 16 << 20

F32 = jnp.float32
BF16 = jnp.bfloat16
MESH = pl.DeviceIdType.MESH


def make_table(bin_devices):
    n = np.arange(L)
    angles = (n[:, None] * np.arange(NB)[None, :] % L).astype(np.float32)
    angles = angles * np.float32(2.0 * math.pi / L)
    hann = np.float32(0.5) - np.float32(0.5) * np.cos(
        n.astype(np.float32) * np.float32(2.0 * math.pi / L)
    )
    parts = np.stack([hann[:, None] * np.cos(angles), -(hann[:, None] * np.sin(angles))])
    parts = parts.reshape(2, L, bin_devices, 2, 4)
    return parts.transpose(4, 0, 2, 3, 1).reshape(8, LANES, L).astype(ml_dtypes.bfloat16)


def nt_dot(a, b):
    return lax.dot_general(a, b, (((1,), (1,)), ((), ())), preferred_element_type=F32)


def tn_dot(a, b):
    return lax.dot_general(a, b, (((0,), (0,)), ((), ())), preferred_element_type=F32)


def lane_pick(x, index):
    return jnp.take_along_axis(x, index, axis=1, mode="promise_in_bounds")


def cut_segments(offsets, record, tiles):
    span = tiles.shape[0] // CH
    for t in range(span):
        column = jnp.zeros((CH, LANES), F32)
        if t < TILES:
            column = record[0, :, t * LANES : (t + 1) * LANES].astype(F32)
        tiles[pl.ds(t, CH, stride=span), :] = column
    source = [tiles[pl.ds(c * span, span), :] for c in range(CH)]
    source = jnp.concatenate(source, axis=1).astype(BF16)

    row = lax.broadcasted_iota(jnp.int32, (SEGS, LANES), 0)
    lane = lax.broadcasted_iota(jnp.int32, (SEGS, LANES), 1)
    start = jnp.zeros((SEGS, LANES), jnp.int32)
    for s in range(SEGS):
        start = jnp.where(row == s, offsets[s], start)
    first = jnp.minimum(start >> 7, TILES - STEPS)
    shift = start - first * LANES
    chosen = jnp.concatenate([(first + t == lane)[:, :span] for t in range(STEPS)], axis=0)
    chosen = jnp.where(chosen, 1.0, 0.0).astype(BF16)
    window = jnp.dot(chosen, source, preferred_element_type=F32)
    window = window.reshape(STEPS, SEGS, CH * LANES)
    index = (lane + shift) & (LANES - 1)
    here = lane + shift < LANES
    rows = []
    for c in range(CH):
        turned = [
            lane_pick(window[t, :, c * LANES : (c + 1) * LANES], index) for t in range(STEPS)
        ]
        cut = [jnp.where(here, turned[t], turned[t + 1]) for t in range(STEPS - 1)]
        rows.append(jnp.concatenate(cut, axis=1))
    return jnp.concatenate(rows, axis=0).astype(BF16)


def pack_spectra(rows, table, loads, stage, send):
    rows = jnp.concatenate([rows, rows], axis=0)
    blocks = []
    for g in range(8):
        loads[g].wait()
        blocks.append(nt_dot(table[g], rows))
    group = lax.broadcasted_iota(jnp.int32, (LANES, LANES), 1) // SEGS
    turned = []
    for r in range(4):
        mixed = blocks[r]
        for q in range(1, 8):
            mixed = jnp.where(group == q, blocks[(q + r) % 8], mixed)
        turned.append(pltpu.roll(mixed, SEGS * r, axis=1) if r else mixed)
    phase = lax.rem(group, 4)
    for c in range(CH):
        out = turned[(0 - c) % 4]
        for g in range(1, 4):
            out = jnp.where(phase == g, turned[(g - c) % 4], out)
        stage[pl.ds(c, LANES, stride=CH), :] = out
    send[...] = stage[...].reshape(send.shape).astype(BF16)


def pick_references(ref_index, recv):
    shape = (2 * REFS, recv.shape[0] * BINS)
    row = lax.broadcasted_iota(jnp.int32, shape, 0)
    col = lax.broadcasted_iota(jnp.int32, shape, 1)
    wanted = jnp.full((2 * REFS, 1), -1, jnp.int32)
    slot = lax.broadcasted_iota(jnp.int32, (2 * REFS, 1), 0)
    for i in range(REFS):
        wanted = jnp.where(lax.rem(slot, REFS) == i, ref_index[0, i], wanted)
    place = (wanted // CH) * BINS + lax.rem(wanted, CH) + (row // REFS) * CH
    chosen = jnp.where(col == place, 1.0, 0.0).astype(BF16)
    rows = recv[...].astype(F32).reshape(shape[1], LANES).astype(BF16)
    return jnp.dot(chosen, rows, preferred_element_type=F32).astype(BF16)


def bin_of(rank):
    return (rank // 32) * 32 + lax.rem(rank, 16) * 2 + lax.rem(rank // 16, 2)


def rank_of(index):
    return (index // 32) * 32 + lax.rem(index, 2) * 16 + lax.rem(index // 2, 16)


def exchange_kernel(
    offsets_hbm,
    ref_index_hbm,
    record_hbm,
    table_hbm,
    recv,
    refs,
    offsets,
    ref_index,
    record,
    table,
    tiles,
    stage,
    send,
    sems,
    table_sems,
    bin_in,
    grp_in,
):
    bins, grps = lax.axis_size("bin"), lax.axis_size("grp")
    me, grp = lax.axis_index("bin"), lax.axis_index("grp")
    rank = rank_of(me)
    load_offsets = pltpu.make_async_copy(offsets_hbm, offsets, sems.at[0])
    load_record = pltpu.make_async_copy(record_hbm, record, sems.at[5])
    load_refs = pltpu.make_async_copy(ref_index_hbm, ref_index, sems.at[6])
    loads = [
        pltpu.make_async_copy(table_hbm.at[g], table.at[g], table_sems.at[g]) for g in range(8)
    ]
    for load in (load_record, load_offsets, *loads, load_refs):
        load.start()

    barrier = pltpu.get_barrier_semaphore()

    @pl.loop(0, bins - 1 - rank)
    def _(k):
        peer = bin_of(bins - 1 - k)
        pl.semaphore_signal(barrier, 1, device_id={"bin": peer}, device_id_type=MESH)

    @pl.loop(grp + 1, grps)
    def _(peer):
        pl.semaphore_signal(barrier, 1, device_id={"grp": peer}, device_id_type=MESH)

    load_offsets.wait()
    load_record.wait()
    rows = cut_segments(offsets, record, tiles)
    pack_spectra(rows, table, loads, stage, send)

    @pl.when(rank + grp > 0)
    def _():
        pl.semaphore_wait(barrier, rank + grp)

    def send_to(peer):
        pltpu.make_async_remote_copy(
            src_ref=send.at[peer],
            dst_ref=recv.at[me],
            send_sem=sems.at[1],
            recv_sem=sems.at[2],
            device_id={"bin": peer},
            device_id_type=MESH,
        ).start()

    @pl.loop(0, rank)
    def _(k):
        peer = bin_of(k)
        send_to(peer)
        pl.semaphore_signal(bin_in.at[me], 1, device_id={"bin": peer}, device_id_type=MESH)

    @pl.loop(0, grp)
    def _(peer):
        pl.semaphore_signal(grp_in.at[grp], 1, device_id={"grp": peer}, device_id_type=MESH)

    recv[pl.ds(me, 1)] = send[pl.ds(me, 1)]

    @pl.loop(rank + 1, bins)
    def _(k):
        peer = bin_of(k)
        pl.semaphore_wait(bin_in.at[peer], 1)
        send_to(peer)

    @pl.loop(grp + 1, grps)
    def _(peer):
        pl.semaphore_wait(grp_in.at[peer], 1)

    load_refs.wait()
    others = recv.at[pl.ds(0, bins - 1)]
    pltpu.make_async_copy(others, others, sems.at[2]).wait()
    refs[pl.ds(grp, 1)] = pick_references(ref_index, recv).reshape(1, 2, REFS, LANES)

    @pl.loop(1, grps)
    def _(k):
        peer = lax.rem(grp + k, grps)
        pltpu.make_async_remote_copy(
            src_ref=refs.at[grp],
            dst_ref=refs.at[grp],
            send_sem=sems.at[3],
            recv_sem=sems.at[4],
            device_id={"grp": peer},
            device_id_type=MESH,
        ).start()

    sent = send.at[pl.ds(0, bins - 1)]
    pltpu.make_async_copy(sent, sent, sems.at[1]).wait()
    other_refs = refs.at[pl.ds(0, grps - 1)]
    pltpu.make_async_copy(other_refs, other_refs, sems.at[4]).wait()
    pltpu.make_async_copy(other_refs, other_refs, sems.at[3]).wait()


def turn(x, imag):
    back = pltpu.roll(x, LANES - SEGS, axis=1)
    ahead = pltpu.roll(x, SEGS, axis=1)
    return jnp.where(imag, ahead, -back)


def invert(z, lane, row):
    imag = lax.rem(lane, 32) >= SEGS
    inner = lax.rem(lane, 32)
    base = lane - inner
    segment = lax.rem(row, SEGS)
    for k in range(SEGS):
        col_re = lane_pick(z, base + k)
        col_im = lane_pick(z, base + (SEGS + k))
        pivot_row = jnp.concatenate(
            [
                jnp.broadcast_to(z[h * SEGS + k : h * SEGS + k + 1], (SEGS, LANES))
                for h in range(2)
            ],
            axis=0,
        )
        pivot = jnp.concatenate(
            [
                jnp.broadcast_to(col_re[h * SEGS + k : h * SEGS + k + 1], (SEGS, LANES))
                for h in range(2)
            ],
            axis=0,
        )
        inverse = 1.0 / pivot
        in_col = lax.rem(lane, SEGS) == k
        unit = jnp.where(inner == k, 1.0, 0.0)
        pivot_row = jnp.where(in_col, unit, pivot_row)
        scaled = pivot_row * inverse
        turned = turn(scaled, imag)
        is_row = segment == k
        col_re = jnp.where(is_row, -1.0, col_re)
        col_im = jnp.where(is_row, 0.0, col_im)
        rest = jnp.where(is_row | in_col, 0.0, z)
        z = rest - col_re * scaled - col_im * turned
    return z


def split(x):
    hi = x.astype(BF16)
    return hi, (x - hi.astype(F32)).astype(BF16)


def solve_kernel(recv, refs, out, flat, chans, result, sems):
    sources = recv.shape[0]
    ranks = refs.shape[0] * REFS
    flat[...] = recv[...].astype(F32).reshape(flat.shape)
    for h in range(2):
        for c in range(CH):
            chans[h, pl.ds(c, sources, stride=CH), :] = flat[
                pl.ds(h * CH + c, sources, stride=BINS), :
            ]

    lane = lax.broadcasted_iota(jnp.int32, (LANES, LANES), 1)
    row = lax.broadcasted_iota(jnp.int32, (LANES, LANES), 0)
    same = (lane // 32) == (row // 32)
    lane32, row32 = lane[:32], row[:32]
    inner32 = lax.rem(lane32, 32)
    blocks, grams, ridges = [], [], []
    for h in range(2):
        x = refs[:, h].reshape(ranks, LANES).astype(F32)
        imag = lax.rem(lax.broadcasted_iota(jnp.int32, x.shape, 1), 32) >= SEGS
        block = jnp.concatenate([x, turn(x, imag)], axis=0).astype(BF16)
        blocks.append(block)
        gram = jnp.where(same, tn_dot(block, block), 0.0)
        gram = gram[0:32] + gram[32:64] + gram[64:96] + gram[96:128]
        diagonal = jnp.where(inner32 == row32, gram, 0.0)
        diagonal = jnp.sum(diagonal, axis=0, keepdims=True)
        group_ones = jnp.where(same, 1.0, 0.0)
        trace = jnp.dot(
            jnp.broadcast_to(diagonal, (8, LANES)),
            group_ones,
            precision=lax.Precision.HIGHEST,
            preferred_element_type=F32,
        )
        ridge = (RIDGE / (2 * ranks)) * trace[:1]
        grams.append(gram[:SEGS] + jnp.where(inner32[:SEGS] == row32[:SEGS], ridge, 0.0))

    inverses = invert(jnp.concatenate(grams, axis=0), lane32, row32)
    imag16 = lax.rem(lane[:SEGS], 32) >= SEGS
    copies = []
    for h in range(2):
        upper = inverses[h * SEGS : (h + 1) * SEGS]
        full = jnp.concatenate([upper, turn(upper, imag16)], axis=0)
        full = jnp.where(same, jnp.concatenate([full] * 4, axis=0), 0.0)
        hi, lo = split(full)
        solved = nt_dot(hi, blocks[h]) + nt_dot(lo, blocks[h])
        y = chans[h].astype(BF16)
        y = jnp.concatenate([y, y], axis=1)
        owner = lax.broadcasted_iota(jnp.int32, solved.shape, 0) // 32
        for b in range(4):
            hi, lo = split(jnp.where(owner == b, solved, 0.0))
            weights = jnp.concatenate([hi, lo], axis=0)
            f = h * 4 + b
            result[f] = jnp.dot(y, weights, preferred_element_type=F32).astype(BF16)
            copy = pltpu.make_async_copy(result.at[f], out.at[f], sems.at[f])
            copy.start()
            copies.append(copy)
    for copy in copies:
        copy.wait()


def in_hbm(x):
    return pltpu.with_memory_space_constraint(x, pltpu.HBM)


def exchange(record, ref_index, offsets, table):
    bins, grps = lax.axis_size("bin"), lax.axis_size("grp")
    vmem = pl.BlockSpec(memory_space=pltpu.VMEM)
    hbm = pl.BlockSpec(memory_space=pltpu.HBM)
    return pl.pallas_call(
        exchange_kernel,
        out_shape=(
            jax.ShapeDtypeStruct((bins, BINS, LANES), BF16),
            jax.ShapeDtypeStruct((grps, 2, REFS, LANES), BF16),
        ),
        in_specs=[hbm, hbm, hbm, hbm],
        out_specs=(vmem, vmem),
        scratch_shapes=[
            pltpu.SMEM(offsets.shape, jnp.int32),
            pltpu.SMEM(ref_index.shape, jnp.int32),
            pltpu.VMEM(record.shape, BF16),
            pltpu.VMEM(table.shape, BF16),
            pltpu.VMEM((CH * 72, LANES), F32),
            pltpu.VMEM((2 * CH * bins, LANES), F32),
            pltpu.VMEM((bins, BINS, LANES), BF16),
            pltpu.SemaphoreType.DMA((7,)),
            pltpu.SemaphoreType.DMA((8,)),
            pltpu.SemaphoreType.REGULAR((bins,)),
            pltpu.SemaphoreType.REGULAR((grps,)),
        ],
        compiler_params=pltpu.CompilerParams(
            collective_id=0, has_side_effects=True, vmem_limit_bytes=VMEM_LIMIT
        ),
    )(*(in_hbm(x) for x in (offsets, ref_index, record, table)))


def solve(recv, refs):
    sources = recv.shape[0]
    chans = sources * CH
    vmem = pl.BlockSpec(memory_space=pltpu.VMEM)
    width = 2 * refs.shape[0] * REFS
    return pl.pallas_call(
        solve_kernel,
        out_shape=jax.ShapeDtypeStruct((BINS, chans, width), BF16),
        in_specs=[vmem, vmem],
        out_specs=pl.BlockSpec(memory_space=pl.ANY),
        scratch_shapes=[
            pltpu.VMEM((sources * BINS, LANES), F32),
            pltpu.VMEM((2, chans, LANES), F32),
            pltpu.VMEM((BINS, chans, width), BF16),
            pltpu.SemaphoreType.DMA((BINS,)),
        ],
        compiler_params=pltpu.CompilerParams(vmem_limit_bytes=VMEM_LIMIT),
    )(recv, refs)


def local(record, ref_index, offsets):
    table = jnp.asarray(make_table(lax.axis_size("bin")))
    recv, refs = exchange(record, ref_index, offsets, table)
    return solve(recv, refs)


def solution(mesh):
    placed = (P("grp", "bin", None), P("grp", None), P())
    return jax.shard_map(
        local, mesh=mesh, in_specs=placed, out_specs=P("bin", "grp", None), check_vma=False
    )
```

```python
import math

import jax
import jax.numpy as jnp
import ml_dtypes
import numpy as np
from jax import lax
from jax.experimental import pallas as pl
from jax.experimental.pallas import tpu as pltpu
from jax.sharding import PartitionSpec as P

L = 1024
NB = 512
SEGS = 16
CH = 4
BINS = 8
REFS = 16
LANES = 128
TILES = 8704 // LANES
STEPS = L // LANES + 1
RIDGE = 0.5
VMEM_LIMIT = 16 << 20

F32 = jnp.float32
BF16 = jnp.bfloat16
MESH = pl.DeviceIdType.MESH


def make_table(bin_devices):
    n = np.arange(L)
    angles = (n[:, None] * np.arange(NB)[None, :] % L).astype(np.float32)
    angles = angles * np.float32(2.0 * math.pi / L)
    hann = np.float32(0.5) - np.float32(0.5) * np.cos(
        n.astype(np.float32) * np.float32(2.0 * math.pi / L)
    )
    parts = np.stack([hann[:, None] * np.cos(angles), -(hann[:, None] * np.sin(angles))])
    parts = parts.reshape(2, L, bin_devices, 2, 4)
    return parts.transpose(4, 0, 2, 3, 1).reshape(8, LANES, L).astype(ml_dtypes.bfloat16)


def nt_dot(a, b):
    return lax.dot_general(a, b, (((1,), (1,)), ((), ())), preferred_element_type=F32)


def tn_dot(a, b):
    return lax.dot_general(a, b, (((0,), (0,)), ((), ())), preferred_element_type=F32)


def lane_pick(x, index):
    return jnp.take_along_axis(x, index, axis=1, mode="promise_in_bounds")


def cut_segments(offsets, record, tiles):
    span = tiles.shape[0] // CH
    for t in range(span):
        column = jnp.zeros((CH, LANES), F32)
        if t < TILES:
            column = record[0, :, t * LANES : (t + 1) * LANES].astype(F32)
        tiles[pl.ds(t, CH, stride=span), :] = column
    source = [tiles[pl.ds(c * span, span), :] for c in range(CH)]
    source = jnp.concatenate(source, axis=1).astype(BF16)

    row = lax.broadcasted_iota(jnp.int32, (SEGS, LANES), 0)
    lane = lax.broadcasted_iota(jnp.int32, (SEGS, LANES), 1)
    start = jnp.zeros((SEGS, LANES), jnp.int32)
    for s in range(SEGS):
        start = jnp.where(row == s, offsets[s], start)
    first = jnp.minimum(start >> 7, TILES - STEPS)
    shift = start - first * LANES
    chosen = jnp.concatenate([(first + t == lane)[:, :span] for t in range(STEPS)], axis=0)
    chosen = jnp.where(chosen, 1.0, 0.0).astype(BF16)
    window = jnp.dot(chosen, source, preferred_element_type=F32)
    window = window.reshape(STEPS, SEGS, CH * LANES)
    index = (lane + shift) & (LANES - 1)
    here = lane + shift < LANES
    rows = []
    for c in range(CH):
        turned = [
            lane_pick(window[t, :, c * LANES : (c + 1) * LANES], index) for t in range(STEPS)
        ]
        cut = [jnp.where(here, turned[t], turned[t + 1]) for t in range(STEPS - 1)]
        rows.append(jnp.concatenate(cut, axis=1))
    return jnp.concatenate(rows, axis=0).astype(BF16)


def pack_spectra(rows, table, loads, stage, send):
    rows = jnp.concatenate([rows, rows], axis=0)
    blocks = []
    for g in range(8):
        loads[g].wait()
        blocks.append(nt_dot(table[g], rows))
    group = lax.broadcasted_iota(jnp.int32, (LANES, LANES), 1) // SEGS
    turned = []
    for r in range(4):
        mixed = blocks[r]
        for q in range(1, 8):
            mixed = jnp.where(group == q, blocks[(q + r) % 8], mixed)
        turned.append(pltpu.roll(mixed, SEGS * r, axis=1) if r else mixed)
    phase = lax.rem(group, 4)
    for c in range(CH):
        out = turned[(0 - c) % 4]
        for g in range(1, 4):
            out = jnp.where(phase == g, turned[(g - c) % 4], out)
        stage[pl.ds(c, LANES, stride=CH), :] = out
    send[...] = stage[...].reshape(send.shape).astype(BF16)


def pick_references(ref_index, recv):
    shape = (2 * REFS, recv.shape[0] * BINS)
    row = lax.broadcasted_iota(jnp.int32, shape, 0)
    col = lax.broadcasted_iota(jnp.int32, shape, 1)
    wanted = jnp.full((2 * REFS, 1), -1, jnp.int32)
    slot = lax.broadcasted_iota(jnp.int32, (2 * REFS, 1), 0)
    for i in range(REFS):
        wanted = jnp.where(lax.rem(slot, REFS) == i, ref_index[0, i], wanted)
    place = (wanted // CH) * BINS + lax.rem(wanted, CH) + (row // REFS) * CH
    chosen = jnp.where(col == place, 1.0, 0.0).astype(BF16)
    rows = recv[...].astype(F32).reshape(shape[1], LANES).astype(BF16)
    return jnp.dot(chosen, rows, preferred_element_type=F32).astype(BF16)


def bin_of(rank):
    return (rank // 32) * 32 + lax.rem(rank, 16) * 2 + lax.rem(rank // 16, 2)


def rank_of(index):
    return (index // 32) * 32 + lax.rem(index, 2) * 16 + lax.rem(index // 2, 16)


def exchange_kernel(
    offsets_hbm,
    ref_index_hbm,
    record_hbm,
    table_hbm,
    recv,
    refs,
    offsets,
    ref_index,
    record,
    table,
    tiles,
    stage,
    send,
    sems,
    table_sems,
    bin_in,
    grp_in,
):
    bins, grps = lax.axis_size("bin"), lax.axis_size("grp")
    me, grp = lax.axis_index("bin"), lax.axis_index("grp")
    rank = rank_of(me)
    load_offsets = pltpu.make_async_copy(offsets_hbm, offsets, sems.at[0])
    load_record = pltpu.make_async_copy(record_hbm, record, sems.at[5])
    load_refs = pltpu.make_async_copy(ref_index_hbm, ref_index, sems.at[6])
    loads = [
        pltpu.make_async_copy(table_hbm.at[g], table.at[g], table_sems.at[g]) for g in range(8)
    ]
    for load in (load_record, load_offsets, *loads, load_refs):
        load.start()

    barrier = pltpu.get_barrier_semaphore()

    @pl.loop(0, bins - 1 - rank)
    def _(k):
        peer = bin_of(bins - 1 - k)
        pl.semaphore_signal(barrier, 1, device_id={"bin": peer}, device_id_type=MESH)

    @pl.loop(grp + 1, grps)
    def _(peer):
        pl.semaphore_signal(barrier, 1, device_id={"grp": peer}, device_id_type=MESH)

    load_offsets.wait()
    load_record.wait()
    rows = cut_segments(offsets, record, tiles)
    pack_spectra(rows, table, loads, stage, send)

    @pl.when(rank + grp > 0)
    def _():
        pl.semaphore_wait(barrier, rank + grp)

    def send_to(peer):
        pltpu.make_async_remote_copy(
            src_ref=send.at[peer],
            dst_ref=recv.at[me],
            send_sem=sems.at[1],
            recv_sem=sems.at[2],
            device_id={"bin": peer},
            device_id_type=MESH,
        ).start()

    @pl.loop(0, rank)
    def _(k):
        peer = bin_of(k)
        send_to(peer)
        pl.semaphore_signal(bin_in.at[me], 1, device_id={"bin": peer}, device_id_type=MESH)

    @pl.loop(0, grp)
    def _(peer):
        pl.semaphore_signal(grp_in.at[grp], 1, device_id={"grp": peer}, device_id_type=MESH)

    recv[pl.ds(me, 1)] = send[pl.ds(me, 1)]

    @pl.loop(rank + 1, bins)
    def _(k):
        peer = bin_of(k)
        pl.semaphore_wait(bin_in.at[peer], 1)
        send_to(peer)

    @pl.loop(grp + 1, grps)
    def _(peer):
        pl.semaphore_wait(grp_in.at[peer], 1)

    load_refs.wait()
    others = recv.at[pl.ds(0, bins - 1)]
    pltpu.make_async_copy(others, others, sems.at[2]).wait()
    refs[pl.ds(grp, 1)] = pick_references(ref_index, recv).reshape(1, 2, REFS, LANES)

    @pl.loop(1, grps)
    def _(k):
        peer = lax.rem(grp + k, grps)
        pltpu.make_async_remote_copy(
            src_ref=refs.at[grp],
            dst_ref=refs.at[grp],
            send_sem=sems.at[3],
            recv_sem=sems.at[4],
            device_id={"grp": peer},
            device_id_type=MESH,
        ).start()

    sent = send.at[pl.ds(0, bins - 1)]
    pltpu.make_async_copy(sent, sent, sems.at[1]).wait()
    other_refs = refs.at[pl.ds(0, grps - 1)]
    pltpu.make_async_copy(other_refs, other_refs, sems.at[4]).wait()
    pltpu.make_async_copy(other_refs, other_refs, sems.at[3]).wait()


def turn(x, imag):
    back = pltpu.roll(x, LANES - SEGS, axis=1)
    ahead = pltpu.roll(x, SEGS, axis=1)
    return jnp.where(imag, ahead, -back)


def invert(z, lane, row):
    inner = lax.rem(lane, 32)
    base = lane - inner
    column = lax.rem(lane, SEGS)
    segment = lax.rem(row, SEGS)
    few = slice(0, 2)
    imag, base2 = inner[few] >= SEGS, base[few]

    def pivot_row(k):
        return jnp.concatenate([z[k : k + 1], z[SEGS + k : SEGS + k + 1]], axis=0)

    def spread(x):
        return jnp.concatenate(
            [jnp.broadcast_to(x[h : h + 1], (SEGS, LANES)) for h in range(2)], axis=0
        )

    for k in range(0, SEGS, 2):
        m = k + 1
        in_cols = (column == k) | (column == m)
        r0, r1 = pivot_row(k), pivot_row(m)
        a = lane_pick(r0, base2 + k)
        b_re = lane_pick(r0, base2 + m)
        b_im = lane_pick(r0, base2 + (SEGS + m))
        d = lane_pick(r1, base2 + m)
        inverse = 1.0 / (a * d - (b_re * b_re + b_im * b_im))
        a, d, b_re, b_im = a * inverse, d * inverse, b_re * inverse, b_im * inverse
        e0 = jnp.where(in_cols[few], jnp.where(inner[few] == k, 1.0, 0.0), r0)
        e1 = jnp.where(in_cols[few], jnp.where(inner[few] == m, 1.0, 0.0), r1)
        t0, t1 = turn(e0, imag), turn(e1, imag)
        w0 = spread(d * e0 - b_re * e1 - b_im * t1)
        w1 = spread(a * e1 - b_re * e0 + b_im * t0)
        tw0 = spread(d * t0 - b_re * t1 + b_im * e1)
        tw1 = spread(a * t1 - b_re * t0 - b_im * e0)
        is0, is1 = segment == k, segment == m
        is_row = is0 | is1
        c0_re = jnp.where(is_row, jnp.where(is0, -1.0, 0.0), lane_pick(z, base + k))
        c0_im = jnp.where(is_row, 0.0, lane_pick(z, base + (SEGS + k)))
        c1_re = jnp.where(is_row, jnp.where(is1, -1.0, 0.0), lane_pick(z, base + m))
        c1_im = jnp.where(is_row, 0.0, lane_pick(z, base + (SEGS + m)))
        rest = jnp.where(is_row | in_cols, 0.0, z)
        z = rest - (c0_re * w0 + c0_im * tw0) - (c1_re * w1 + c1_im * tw1)
    return z


def split(x):
    hi = x.astype(BF16)
    return hi, (x - hi.astype(F32)).astype(BF16)


def solve_kernel(recv, refs, out, flat, chans, result, sems):
    sources = recv.shape[0]
    ranks = refs.shape[0] * REFS
    flat[...] = recv[...].astype(F32).reshape(flat.shape)
    for h in range(2):
        for c in range(CH):
            chans[h, pl.ds(c, sources, stride=CH), :] = flat[
                pl.ds(h * CH + c, sources, stride=BINS), :
            ]

    lane = lax.broadcasted_iota(jnp.int32, (LANES, LANES), 1)
    row = lax.broadcasted_iota(jnp.int32, (LANES, LANES), 0)
    same = (lane // 32) == (row // 32)
    lane32, row32 = lane[:32], row[:32]
    inner32 = lax.rem(lane32, 32)
    blocks, grams, ridges = [], [], []
    for h in range(2):
        x = refs[:, h].reshape(ranks, LANES).astype(F32)
        imag = lax.rem(lax.broadcasted_iota(jnp.int32, x.shape, 1), 32) >= SEGS
        block = jnp.concatenate([x, turn(x, imag)], axis=0).astype(BF16)
        blocks.append(block)
        gram = jnp.where(same, tn_dot(block, block), 0.0)
        gram = gram[0:32] + gram[32:64] + gram[64:96] + gram[96:128]
        diagonal = jnp.where(inner32 == row32, gram, 0.0)
        diagonal = jnp.sum(diagonal, axis=0, keepdims=True)
        group_ones = jnp.where(same, 1.0, 0.0)
        trace = jnp.dot(
            jnp.broadcast_to(diagonal, (8, LANES)),
            group_ones,
            precision=lax.Precision.HIGHEST,
            preferred_element_type=F32,
        )
        ridge = (RIDGE / (2 * ranks)) * trace[:1]
        grams.append(gram[:SEGS] + jnp.where(inner32[:SEGS] == row32[:SEGS], ridge, 0.0))

    inverses = invert(jnp.concatenate(grams, axis=0), lane32, row32)
    imag16 = lax.rem(lane[:SEGS], 32) >= SEGS
    copies = []
    for h in range(2):
        upper = inverses[h * SEGS : (h + 1) * SEGS]
        full = jnp.concatenate([upper, turn(upper, imag16)], axis=0)
        full = jnp.where(same, jnp.concatenate([full] * 4, axis=0), 0.0)
        hi, lo = split(full)
        solved = nt_dot(hi, blocks[h]) + nt_dot(lo, blocks[h])
        y = chans[h].astype(BF16)
        y = jnp.concatenate([y, y], axis=1)
        owner = lax.broadcasted_iota(jnp.int32, solved.shape, 0) // 32
        for b in range(4):
            hi, lo = split(jnp.where(owner == b, solved, 0.0))
            weights = jnp.concatenate([hi, lo], axis=0)
            f = h * 4 + b
            result[f] = jnp.dot(y, weights, preferred_element_type=F32).astype(BF16)
            copy = pltpu.make_async_copy(result.at[f], out.at[f], sems.at[f])
            copy.start()
            copies.append(copy)
    for copy in copies:
        copy.wait()


def in_hbm(x):
    return pltpu.with_memory_space_constraint(x, pltpu.HBM)


def exchange(record, ref_index, offsets, table):
    bins, grps = lax.axis_size("bin"), lax.axis_size("grp")
    vmem = pl.BlockSpec(memory_space=pltpu.VMEM)
    hbm = pl.BlockSpec(memory_space=pltpu.HBM)
    return pl.pallas_call(
        exchange_kernel,
        out_shape=(
            jax.ShapeDtypeStruct((bins, BINS, LANES), BF16),
            jax.ShapeDtypeStruct((grps, 2, REFS, LANES), BF16),
        ),
        in_specs=[hbm, hbm, hbm, hbm],
        out_specs=(vmem, vmem),
        scratch_shapes=[
            pltpu.SMEM(offsets.shape, jnp.int32),
            pltpu.SMEM(ref_index.shape, jnp.int32),
            pltpu.VMEM(record.shape, BF16),
            pltpu.VMEM(table.shape, BF16),
            pltpu.VMEM((CH * 72, LANES), F32),
            pltpu.VMEM((2 * CH * bins, LANES), F32),
            pltpu.VMEM((bins, BINS, LANES), BF16),
            pltpu.SemaphoreType.DMA((7,)),
            pltpu.SemaphoreType.DMA((8,)),
            pltpu.SemaphoreType.REGULAR((bins,)),
            pltpu.SemaphoreType.REGULAR((grps,)),
        ],
        compiler_params=pltpu.CompilerParams(
            collective_id=0, has_side_effects=True, vmem_limit_bytes=VMEM_LIMIT
        ),
    )(*(in_hbm(x) for x in (offsets, ref_index, record, table)))


def solve(recv, refs):
    sources = recv.shape[0]
    chans = sources * CH
    vmem = pl.BlockSpec(memory_space=pltpu.VMEM)
    width = 2 * refs.shape[0] * REFS
    return pl.pallas_call(
        solve_kernel,
        out_shape=jax.ShapeDtypeStruct((BINS, chans, width), BF16),
        in_specs=[vmem, vmem],
        out_specs=pl.BlockSpec(memory_space=pl.ANY),
        scratch_shapes=[
            pltpu.VMEM((sources * BINS, LANES), F32),
            pltpu.VMEM((2, chans, LANES), F32),
            pltpu.VMEM((BINS, chans, width), BF16),
            pltpu.SemaphoreType.DMA((BINS,)),
        ],
        compiler_params=pltpu.CompilerParams(vmem_limit_bytes=VMEM_LIMIT),
    )(recv, refs)


def local(record, ref_index, offsets):
    table = jnp.asarray(make_table(lax.axis_size("bin")))
    recv, refs = exchange(record, ref_index, offsets, table)
    return solve(recv, refs)


def solution(mesh):
    placed = (P("grp", "bin", None), P("grp", None), P())
    return jax.shard_map(
        local, mesh=mesh, in_specs=placed, out_specs=P("bin", "grp", None), check_vma=False
    )
```

```python
import math

import jax
import jax.numpy as jnp
import ml_dtypes
import numpy as np
from jax import lax
from jax.experimental import pallas as pl
from jax.experimental.pallas import tpu as pltpu
from jax.sharding import PartitionSpec as P

L = 1024
NB = 512
SEGS = 16
CH = 4
BINS = 8
REFS = 16
LANES = 128
TILES = 8704 // LANES
STEPS = L // LANES + 1
RIDGE = 0.5
VMEM_LIMIT = 16 << 20

F32 = jnp.float32
BF16 = jnp.bfloat16
MESH = pl.DeviceIdType.MESH


def make_table(bin_devices):
    n = np.arange(L)
    angles = (n[:, None] * np.arange(NB)[None, :] % L).astype(np.float32)
    angles = angles * np.float32(2.0 * math.pi / L)
    hann = np.float32(0.5) - np.float32(0.5) * np.cos(
        n.astype(np.float32) * np.float32(2.0 * math.pi / L)
    )
    parts = np.stack([hann[:, None] * np.cos(angles), -(hann[:, None] * np.sin(angles))])
    parts = parts.reshape(2, L, bin_devices, 2, 4)
    return parts.transpose(4, 0, 2, 3, 1).reshape(8, LANES, L).astype(ml_dtypes.bfloat16)


def nt_dot(a, b):
    return lax.dot_general(a, b, (((1,), (1,)), ((), ())), preferred_element_type=F32)


def tn_dot(a, b):
    return lax.dot_general(a, b, (((0,), (0,)), ((), ())), preferred_element_type=F32)


def lane_pick(x, index):
    return jnp.take_along_axis(x, index, axis=1, mode="promise_in_bounds")


def cut_segments(offsets, record, tiles):
    span = tiles.shape[0] // CH
    for t in range(span):
        column = jnp.zeros((CH, LANES), F32)
        if t < TILES:
            column = record[0, :, t * LANES : (t + 1) * LANES].astype(F32)
        tiles[pl.ds(t, CH, stride=span), :] = column
    source = [tiles[pl.ds(c * span, span), :] for c in range(CH)]
    source = jnp.concatenate(source, axis=1).astype(BF16)

    row = lax.broadcasted_iota(jnp.int32, (SEGS, LANES), 0)
    lane = lax.broadcasted_iota(jnp.int32, (SEGS, LANES), 1)
    start = jnp.zeros((SEGS, LANES), jnp.int32)
    for s in range(SEGS):
        start = jnp.where(row == s, offsets[s], start)
    first = jnp.minimum(start >> 7, TILES - STEPS)
    shift = start - first * LANES
    chosen = jnp.concatenate([(first + t == lane)[:, :span] for t in range(STEPS)], axis=0)
    chosen = jnp.where(chosen, 1.0, 0.0).astype(BF16)
    window = jnp.dot(chosen, source, preferred_element_type=F32)
    window = window.reshape(STEPS, SEGS, CH * LANES)
    index = (lane + shift) & (LANES - 1)
    here = lane + shift < LANES
    rows = []
    for c in range(CH):
        turned = [
            lane_pick(window[t, :, c * LANES : (c + 1) * LANES], index) for t in range(STEPS)
        ]
        cut = [jnp.where(here, turned[t], turned[t + 1]) for t in range(STEPS - 1)]
        rows.append(jnp.concatenate(cut, axis=1))
    return jnp.concatenate(rows, axis=0).astype(BF16)


def pack_spectra(rows, table, loads, stage, send):
    rows = jnp.concatenate([rows, rows], axis=0)
    blocks = []
    for g in range(8):
        loads[g].wait()
        blocks.append(nt_dot(table[g], rows))
    group = lax.broadcasted_iota(jnp.int32, (LANES, LANES), 1) // SEGS
    turned = []
    for r in range(4):
        mixed = blocks[r]
        for q in range(1, 8):
            mixed = jnp.where(group == q, blocks[(q + r) % 8], mixed)
        turned.append(pltpu.roll(mixed, SEGS * r, axis=1) if r else mixed)
    phase = lax.rem(group, 4)
    for c in range(CH):
        out = turned[(0 - c) % 4]
        for g in range(1, 4):
            out = jnp.where(phase == g, turned[(g - c) % 4], out)
        stage[pl.ds(c, LANES, stride=CH), :] = out
    send[...] = stage[...].reshape(send.shape).astype(BF16)


def pick_references(ref_index, recv):
    shape = (2 * REFS, recv.shape[0] * BINS)
    row = lax.broadcasted_iota(jnp.int32, shape, 0)
    col = lax.broadcasted_iota(jnp.int32, shape, 1)
    wanted = jnp.full((2 * REFS, 1), -1, jnp.int32)
    slot = lax.broadcasted_iota(jnp.int32, (2 * REFS, 1), 0)
    for i in range(REFS):
        wanted = jnp.where(lax.rem(slot, REFS) == i, ref_index[0, i], wanted)
    place = (wanted // CH) * BINS + lax.rem(wanted, CH) + (row // REFS) * CH
    chosen = jnp.where(col == place, 1.0, 0.0).astype(BF16)
    rows = recv[...].astype(F32).reshape(shape[1], LANES).astype(BF16)
    return jnp.dot(chosen, rows, preferred_element_type=F32).astype(BF16)


def exchange_kernel(
    offsets_hbm,
    ref_index_hbm,
    record_hbm,
    table_hbm,
    recv,
    refs,
    offsets,
    ref_index,
    record,
    table,
    tiles,
    stage,
    send,
    sems,
    table_sems,
    bin_in,
    grp_in,
):
    bins, grps = lax.axis_size("bin"), lax.axis_size("grp")
    me, grp = lax.axis_index("bin"), lax.axis_index("grp")
    grp_rank = grp + lax.rem(me, 2) * (grps - 1 - 2 * grp)

    def in_grp(k):
        return {"grp": k + lax.rem(me, 2) * (grps - 1 - 2 * k)}

    load_offsets = pltpu.make_async_copy(offsets_hbm, offsets, sems.at[0])
    load_record = pltpu.make_async_copy(record_hbm, record, sems.at[5])
    load_refs = pltpu.make_async_copy(ref_index_hbm, ref_index, sems.at[6])
    loads = [
        pltpu.make_async_copy(table_hbm.at[g], table.at[g], table_sems.at[g]) for g in range(8)
    ]
    for load in (load_record, load_offsets, *loads, load_refs):
        load.start()

    barrier = pltpu.get_barrier_semaphore()

    @pl.loop(0, bins - 1 - me)
    def _(k):
        peer = bins - 1 - k
        pl.semaphore_signal(barrier, 1, device_id={"bin": peer}, device_id_type=MESH)

    @pl.loop(grp_rank + 1, grps)
    def _(k):
        pl.semaphore_signal(barrier, 1, device_id=in_grp(k), device_id_type=MESH)

    load_offsets.wait()
    load_record.wait()
    rows = cut_segments(offsets, record, tiles)
    pack_spectra(rows, table, loads, stage, send)

    before = me + grp_rank

    @pl.when(before > 0)
    def _():
        pl.semaphore_wait(barrier, before)

    def send_to(peer):
        pltpu.make_async_remote_copy(
            src_ref=send.at[peer],
            dst_ref=recv.at[me],
            send_sem=sems.at[1],
            recv_sem=sems.at[2],
            device_id={"bin": peer},
            device_id_type=MESH,
        ).start()

    @pl.loop(0, me)
    def _(peer):
        send_to(peer)
        pl.semaphore_signal(bin_in.at[me], 1, device_id={"bin": peer}, device_id_type=MESH)

    @pl.loop(0, grp_rank)
    def _(k):
        pl.semaphore_signal(grp_in.at[grp_rank], 1, device_id=in_grp(k), device_id_type=MESH)

    recv[pl.ds(me, 1)] = send[pl.ds(me, 1)]

    @pl.loop(me + 1, bins)
    def _(peer):
        pl.semaphore_wait(bin_in.at[peer], 1)
        send_to(peer)

    @pl.loop(grp_rank + 1, grps)
    def _(k):
        pl.semaphore_wait(grp_in.at[k], 1)

    load_refs.wait()
    others = recv.at[pl.ds(0, bins - 1)]
    pltpu.make_async_copy(others, others, sems.at[2]).wait()
    refs[pl.ds(grp, 1)] = pick_references(ref_index, recv).reshape(1, 2, REFS, LANES)

    @pl.loop(1, grps)
    def _(k):
        peer = lax.rem(grp + k, grps)
        pltpu.make_async_remote_copy(
            src_ref=refs.at[grp],
            dst_ref=refs.at[grp],
            send_sem=sems.at[3],
            recv_sem=sems.at[4],
            device_id={"grp": peer},
            device_id_type=MESH,
        ).start()

    sent = send.at[pl.ds(0, bins - 1)]
    pltpu.make_async_copy(sent, sent, sems.at[1]).wait()
    other_refs = refs.at[pl.ds(0, grps - 1)]
    pltpu.make_async_copy(other_refs, other_refs, sems.at[4]).wait()
    pltpu.make_async_copy(other_refs, other_refs, sems.at[3]).wait()


def turn(x, imag):
    back = pltpu.roll(x, LANES - SEGS, axis=1)
    ahead = pltpu.roll(x, SEGS, axis=1)
    return jnp.where(imag, ahead, -back)


def invert(z, lane, row):
    inner = lax.rem(lane, 32)
    base = lane - inner
    column = lax.rem(lane, SEGS)
    segment = lax.rem(row, SEGS)
    few = slice(0, 2)
    imag, base2 = inner[few] >= SEGS, base[few]

    def pivot_row(k):
        return jnp.concatenate([z[k : k + 1], z[SEGS + k : SEGS + k + 1]], axis=0)

    def spread(x):
        return jnp.concatenate(
            [jnp.broadcast_to(x[h : h + 1], (SEGS, LANES)) for h in range(2)], axis=0
        )

    for k in range(0, SEGS, 2):
        m = k + 1
        in_cols = (column == k) | (column == m)
        r0, r1 = pivot_row(k), pivot_row(m)
        a = lane_pick(r0, base2 + k)
        b_re = lane_pick(r0, base2 + m)
        b_im = lane_pick(r0, base2 + (SEGS + m))
        d = lane_pick(r1, base2 + m)
        inverse = 1.0 / (a * d - (b_re * b_re + b_im * b_im))
        a, d, b_re, b_im = a * inverse, d * inverse, b_re * inverse, b_im * inverse
        e0 = jnp.where(in_cols[few], jnp.where(inner[few] == k, 1.0, 0.0), r0)
        e1 = jnp.where(in_cols[few], jnp.where(inner[few] == m, 1.0, 0.0), r1)
        t0, t1 = turn(e0, imag), turn(e1, imag)
        w0 = spread(d * e0 - b_re * e1 - b_im * t1)
        w1 = spread(a * e1 - b_re * e0 + b_im * t0)
        tw0 = spread(d * t0 - b_re * t1 + b_im * e1)
        tw1 = spread(a * t1 - b_re * t0 - b_im * e0)
        is0, is1 = segment == k, segment == m
        is_row = is0 | is1
        c0_re = jnp.where(is_row, jnp.where(is0, -1.0, 0.0), lane_pick(z, base + k))
        c0_im = jnp.where(is_row, 0.0, lane_pick(z, base + (SEGS + k)))
        c1_re = jnp.where(is_row, jnp.where(is1, -1.0, 0.0), lane_pick(z, base + m))
        c1_im = jnp.where(is_row, 0.0, lane_pick(z, base + (SEGS + m)))
        rest = jnp.where(is_row | in_cols, 0.0, z)
        z = rest - (c0_re * w0 + c0_im * tw0) - (c1_re * w1 + c1_im * tw1)
    return z


def split(x):
    hi = x.astype(BF16)
    return hi, (x - hi.astype(F32)).astype(BF16)


def solve_kernel(recv, refs, out, flat, chans, result, sems):
    sources = recv.shape[0]
    ranks = refs.shape[0] * REFS
    flat[...] = recv[...].astype(F32).reshape(flat.shape)
    for h in range(2):
        for c in range(CH):
            chans[h, pl.ds(c, sources, stride=CH), :] = flat[
                pl.ds(h * CH + c, sources, stride=BINS), :
            ]

    lane = lax.broadcasted_iota(jnp.int32, (LANES, LANES), 1)
    row = lax.broadcasted_iota(jnp.int32, (LANES, LANES), 0)
    same = (lane // 32) == (row // 32)
    lane32, row32 = lane[:32], row[:32]
    inner32 = lax.rem(lane32, 32)
    blocks, grams, ridges = [], [], []
    for h in range(2):
        x = refs[:, h].reshape(ranks, LANES).astype(F32)
        imag = lax.rem(lax.broadcasted_iota(jnp.int32, x.shape, 1), 32) >= SEGS
        block = jnp.concatenate([x, turn(x, imag)], axis=0).astype(BF16)
        blocks.append(block)
        gram = jnp.where(same, tn_dot(block, block), 0.0)
        gram = gram[0:32] + gram[32:64] + gram[64:96] + gram[96:128]
        diagonal = jnp.where(inner32 == row32, gram, 0.0)
        diagonal = jnp.sum(diagonal, axis=0, keepdims=True)
        group_ones = jnp.where(same, 1.0, 0.0)
        trace = jnp.dot(
            jnp.broadcast_to(diagonal, (8, LANES)),
            group_ones,
            precision=lax.Precision.HIGHEST,
            preferred_element_type=F32,
        )
        ridge = (RIDGE / (2 * ranks)) * trace[:1]
        grams.append(gram[:SEGS] + jnp.where(inner32[:SEGS] == row32[:SEGS], ridge, 0.0))

    inverses = invert(jnp.concatenate(grams, axis=0), lane32, row32)
    imag16 = lax.rem(lane[:SEGS], 32) >= SEGS
    copies = []
    for h in range(2):
        upper = inverses[h * SEGS : (h + 1) * SEGS]
        full = jnp.concatenate([upper, turn(upper, imag16)], axis=0)
        full = jnp.where(same, jnp.concatenate([full] * 4, axis=0), 0.0)
        hi, lo = split(full)
        solved = nt_dot(hi, blocks[h]) + nt_dot(lo, blocks[h])
        y = chans[h].astype(BF16)
        y = jnp.concatenate([y, y], axis=1)
        owner = lax.broadcasted_iota(jnp.int32, solved.shape, 0) // 32
        for b in range(4):
            hi, lo = split(jnp.where(owner == b, solved, 0.0))
            weights = jnp.concatenate([hi, lo], axis=0)
            f = h * 4 + b
            result[f] = jnp.dot(y, weights, preferred_element_type=F32).astype(BF16)
            copy = pltpu.make_async_copy(result.at[f], out.at[f], sems.at[f])
            copy.start()
            copies.append(copy)
    for copy in copies:
        copy.wait()


def in_hbm(x):
    return pltpu.with_memory_space_constraint(x, pltpu.HBM)


def exchange(record, ref_index, offsets, table):
    bins, grps = lax.axis_size("bin"), lax.axis_size("grp")
    vmem = pl.BlockSpec(memory_space=pltpu.VMEM)
    hbm = pl.BlockSpec(memory_space=pltpu.HBM)
    return pl.pallas_call(
        exchange_kernel,
        out_shape=(
            jax.ShapeDtypeStruct((bins, BINS, LANES), BF16),
            jax.ShapeDtypeStruct((grps, 2, REFS, LANES), BF16),
        ),
        in_specs=[hbm, hbm, hbm, hbm],
        out_specs=(vmem, vmem),
        scratch_shapes=[
            pltpu.SMEM(offsets.shape, jnp.int32),
            pltpu.SMEM(ref_index.shape, jnp.int32),
            pltpu.VMEM(record.shape, BF16),
            pltpu.VMEM(table.shape, BF16),
            pltpu.VMEM((CH * 72, LANES), F32),
            pltpu.VMEM((2 * CH * bins, LANES), F32),
            pltpu.VMEM((bins, BINS, LANES), BF16),
            pltpu.SemaphoreType.DMA((7,)),
            pltpu.SemaphoreType.DMA((8,)),
            pltpu.SemaphoreType.REGULAR((bins,)),
            pltpu.SemaphoreType.REGULAR((grps,)),
        ],
        compiler_params=pltpu.CompilerParams(
            collective_id=0, has_side_effects=True, vmem_limit_bytes=VMEM_LIMIT
        ),
    )(*(in_hbm(x) for x in (offsets, ref_index, record, table)))


def solve(recv, refs):
    sources = recv.shape[0]
    chans = sources * CH
    vmem = pl.BlockSpec(memory_space=pltpu.VMEM)
    width = 2 * refs.shape[0] * REFS
    return pl.pallas_call(
        solve_kernel,
        out_shape=jax.ShapeDtypeStruct((BINS, chans, width), BF16),
        in_specs=[vmem, vmem],
        out_specs=pl.BlockSpec(memory_space=pl.ANY),
        scratch_shapes=[
            pltpu.VMEM((sources * BINS, LANES), F32),
            pltpu.VMEM((2, chans, LANES), F32),
            pltpu.VMEM((BINS, chans, width), BF16),
            pltpu.SemaphoreType.DMA((BINS,)),
        ],
        compiler_params=pltpu.CompilerParams(vmem_limit_bytes=VMEM_LIMIT),
    )(recv, refs)


def local(record, ref_index, offsets):
    table = jnp.asarray(make_table(lax.axis_size("bin")))
    recv, refs = exchange(record, ref_index, offsets, table)
    return solve(recv, refs)


def solution(mesh):
    placed = (P("grp", "bin", None), P("grp", None), P())
    return jax.shard_map(
        local, mesh=mesh, in_specs=placed, out_specs=P("bin", "grp", None), check_vma=False
    )
```

```python
import math

import jax
import jax.numpy as jnp
import ml_dtypes
import numpy as np
from jax import lax
from jax.experimental import pallas as pl
from jax.experimental.pallas import tpu as pltpu
from jax.sharding import PartitionSpec as P

L = 1024
NB = 512
SEGS = 16
CH = 4
BINS = 8
REFS = 16
LANES = 128
TILES = 8704 // LANES
STEPS = L // LANES + 1
RIDGE = 0.5
VMEM_LIMIT = 16 << 20

F32 = jnp.float32
BF16 = jnp.bfloat16
MESH = pl.DeviceIdType.MESH


def make_table(bin_devices):
    n = np.arange(L)
    angles = (n[:, None] * np.arange(NB)[None, :] % L).astype(np.float32)
    angles = angles * np.float32(2.0 * math.pi / L)
    hann = np.float32(0.5) - np.float32(0.5) * np.cos(
        n.astype(np.float32) * np.float32(2.0 * math.pi / L)
    )
    parts = np.stack([hann[:, None] * np.cos(angles), -(hann[:, None] * np.sin(angles))])
    parts = parts.reshape(2, L, bin_devices, 2, 4)
    return parts.transpose(4, 0, 2, 3, 1).reshape(8, LANES, L).astype(ml_dtypes.bfloat16)


def nt_dot(a, b):
    return lax.dot_general(a, b, (((1,), (1,)), ((), ())), preferred_element_type=F32)


def tn_dot(a, b):
    return lax.dot_general(a, b, (((0,), (0,)), ((), ())), preferred_element_type=F32)


def lane_pick(x, index):
    return jnp.take_along_axis(x, index, axis=1, mode="promise_in_bounds")


def cut_segments(offsets, record, tiles):
    span = tiles.shape[0] // CH
    for t in range(span):
        column = jnp.zeros((CH, LANES), F32)
        if t < TILES:
            column = record[0, :, t * LANES : (t + 1) * LANES].astype(F32)
        tiles[pl.ds(t, CH, stride=span), :] = column
    source = [tiles[pl.ds(c * span, span), :] for c in range(CH)]
    source = jnp.concatenate(source, axis=1).astype(BF16)

    row = lax.broadcasted_iota(jnp.int32, (SEGS, LANES), 0)
    lane = lax.broadcasted_iota(jnp.int32, (SEGS, LANES), 1)
    start = jnp.zeros((SEGS, LANES), jnp.int32)
    for s in range(SEGS):
        start = jnp.where(row == s, offsets[s], start)
    first = jnp.minimum(start >> 7, TILES - STEPS)
    shift = start - first * LANES
    chosen = jnp.concatenate([(first + t == lane)[:, :span] for t in range(STEPS)], axis=0)
    chosen = jnp.where(chosen, 1.0, 0.0).astype(BF16)
    window = jnp.dot(chosen, source, preferred_element_type=F32)
    window = window.reshape(STEPS, SEGS, CH * LANES)
    index = (lane + shift) & (LANES - 1)
    here = lane + shift < LANES
    rows = []
    for c in range(CH):
        turned = [
            lane_pick(window[t, :, c * LANES : (c + 1) * LANES], index) for t in range(STEPS)
        ]
        cut = [jnp.where(here, turned[t], turned[t + 1]) for t in range(STEPS - 1)]
        rows.append(jnp.concatenate(cut, axis=1))
    return jnp.concatenate(rows, axis=0).astype(BF16)


def pack_spectra(rows, table, loads, stage, send):
    rows = jnp.concatenate([rows, rows], axis=0)
    blocks = []
    for g in range(8):
        loads[g].wait()
        blocks.append(nt_dot(table[g], rows))
    group = lax.broadcasted_iota(jnp.int32, (LANES, LANES), 1) // SEGS
    turned = []
    for r in range(4):
        mixed = blocks[r]
        for q in range(1, 8):
            mixed = jnp.where(group == q, blocks[(q + r) % 8], mixed)
        turned.append(pltpu.roll(mixed, SEGS * r, axis=1) if r else mixed)
    phase = lax.rem(group, 4)
    for c in range(CH):
        out = turned[(0 - c) % 4]
        for g in range(1, 4):
            out = jnp.where(phase == g, turned[(g - c) % 4], out)
        stage[pl.ds(c, LANES, stride=CH), :] = out
    send[...] = stage[...].reshape(send.shape).astype(BF16)


def reference_choice(ref_index, sources):
    shape = (2 * REFS, sources * BINS)
    row = lax.broadcasted_iota(jnp.int32, shape, 0)
    col = lax.broadcasted_iota(jnp.int32, shape, 1)
    wanted = jnp.full((2 * REFS, 1), -1, jnp.int32)
    slot = lax.broadcasted_iota(jnp.int32, (2 * REFS, 1), 0)
    for i in range(REFS):
        wanted = jnp.where(lax.rem(slot, REFS) == i, ref_index[0, i], wanted)
    place = (wanted // CH) * BINS + lax.rem(wanted, CH) + (row // REFS) * CH
    return jnp.where(col == place, 1.0, 0.0).astype(BF16)


def exchange_kernel(
    offsets_hbm,
    ref_index_hbm,
    record_hbm,
    table_hbm,
    recv,
    refs,
    offsets,
    ref_index,
    record,
    table,
    tiles,
    stage,
    send,
    sems,
    table_sems,
    bin_in,
    grp_in,
):
    bins, grps = lax.axis_size("bin"), lax.axis_size("grp")
    me, grp = lax.axis_index("bin"), lax.axis_index("grp")
    grp_rank = grp + lax.rem(me, 2) * (grps - 1 - 2 * grp)

    def in_grp(k):
        return {"grp": k + lax.rem(me, 2) * (grps - 1 - 2 * k)}

    load_offsets = pltpu.make_async_copy(offsets_hbm, offsets, sems.at[0])
    load_record = pltpu.make_async_copy(record_hbm, record, sems.at[5])
    load_refs = pltpu.make_async_copy(ref_index_hbm, ref_index, sems.at[6])
    loads = [
        pltpu.make_async_copy(table_hbm.at[g], table.at[g], table_sems.at[g]) for g in range(8)
    ]
    for load in (load_record, load_offsets, *loads, load_refs):
        load.start()

    barrier = pltpu.get_barrier_semaphore()

    @pl.loop(0, bins - 1 - me)
    def _(k):
        peer = bins - 1 - k
        pl.semaphore_signal(barrier, 1, device_id={"bin": peer}, device_id_type=MESH)

    @pl.loop(grp_rank + 1, grps)
    def _(k):
        pl.semaphore_signal(barrier, 1, device_id=in_grp(k), device_id_type=MESH)

    load_offsets.wait()
    load_record.wait()
    rows = cut_segments(offsets, record, tiles)
    pack_spectra(rows, table, loads, stage, send)

    before = me + grp_rank

    @pl.when(before > 0)
    def _():
        pl.semaphore_wait(barrier, before)

    def send_to(peer):
        pltpu.make_async_remote_copy(
            src_ref=send.at[peer],
            dst_ref=recv.at[me],
            send_sem=sems.at[1],
            recv_sem=sems.at[2],
            device_id={"bin": peer},
            device_id_type=MESH,
        ).start()

    @pl.loop(0, me)
    def _(peer):
        send_to(peer)
        pl.semaphore_signal(bin_in.at[me], 1, device_id={"bin": peer}, device_id_type=MESH)

    @pl.loop(0, grp_rank)
    def _(k):
        pl.semaphore_signal(grp_in.at[grp_rank], 1, device_id=in_grp(k), device_id_type=MESH)

    recv[pl.ds(me, 1)] = send[pl.ds(me, 1)]

    @pl.loop(me + 1, bins)
    def _(peer):
        pl.semaphore_wait(bin_in.at[peer], 1)
        send_to(peer)

    @pl.loop(grp_rank + 1, grps)
    def _(k):
        pl.semaphore_wait(grp_in.at[k], 1)

    load_refs.wait()
    choice = reference_choice(ref_index, bins)
    others = recv.at[pl.ds(0, bins - 1)]
    pltpu.make_async_copy(others, others, sems.at[2]).wait()
    received = recv[...].astype(F32).reshape(bins * BINS, LANES).astype(BF16)
    chosen = jnp.dot(choice, received, preferred_element_type=F32).astype(BF16)
    refs[pl.ds(grp, 1)] = chosen.reshape(1, 2, REFS, LANES)

    @pl.loop(1, grps)
    def _(k):
        peer = lax.rem(grp + k, grps)
        pltpu.make_async_remote_copy(
            src_ref=refs.at[grp],
            dst_ref=refs.at[grp],
            send_sem=sems.at[3],
            recv_sem=sems.at[4],
            device_id={"grp": peer},
            device_id_type=MESH,
        ).start()

    sent = send.at[pl.ds(0, bins - 1)]
    pltpu.make_async_copy(sent, sent, sems.at[1]).wait()
    other_refs = refs.at[pl.ds(0, grps - 1)]
    pltpu.make_async_copy(other_refs, other_refs, sems.at[4]).wait()
    pltpu.make_async_copy(other_refs, other_refs, sems.at[3]).wait()


def turn(x, imag):
    back = pltpu.roll(x, LANES - SEGS, axis=1)
    ahead = pltpu.roll(x, SEGS, axis=1)
    return jnp.where(imag, ahead, -back)


def invert(z, lane, row):
    inner = lax.rem(lane, 32)
    base = lane - inner
    column = lax.rem(lane, SEGS)
    segment = lax.rem(row, SEGS)
    few = slice(0, 2)
    imag, base2 = inner[few] >= SEGS, base[few]

    def pivot_row(k):
        return jnp.concatenate([z[k : k + 1], z[SEGS + k : SEGS + k + 1]], axis=0)

    def spread(x):
        return jnp.concatenate(
            [jnp.broadcast_to(x[h : h + 1], (SEGS, LANES)) for h in range(2)], axis=0
        )

    for k in range(0, SEGS, 2):
        m = k + 1
        in_cols = (column == k) | (column == m)
        r0, r1 = pivot_row(k), pivot_row(m)
        a = lane_pick(r0, base2 + k)
        b_re = lane_pick(r0, base2 + m)
        b_im = lane_pick(r0, base2 + (SEGS + m))
        d = lane_pick(r1, base2 + m)
        inverse = 1.0 / (a * d - (b_re * b_re + b_im * b_im))
        a, d, b_re, b_im = a * inverse, d * inverse, b_re * inverse, b_im * inverse
        e0 = jnp.where(in_cols[few], jnp.where(inner[few] == k, 1.0, 0.0), r0)
        e1 = jnp.where(in_cols[few], jnp.where(inner[few] == m, 1.0, 0.0), r1)
        t0, t1 = turn(e0, imag), turn(e1, imag)
        w0 = spread(d * e0 - b_re * e1 - b_im * t1)
        w1 = spread(a * e1 - b_re * e0 + b_im * t0)
        tw0 = spread(d * t0 - b_re * t1 + b_im * e1)
        tw1 = spread(a * t1 - b_re * t0 - b_im * e0)
        is0, is1 = segment == k, segment == m
        is_row = is0 | is1
        c0_re = jnp.where(is_row, jnp.where(is0, -1.0, 0.0), lane_pick(z, base + k))
        c0_im = jnp.where(is_row, 0.0, lane_pick(z, base + (SEGS + k)))
        c1_re = jnp.where(is_row, jnp.where(is1, -1.0, 0.0), lane_pick(z, base + m))
        c1_im = jnp.where(is_row, 0.0, lane_pick(z, base + (SEGS + m)))
        rest = jnp.where(is_row | in_cols, 0.0, z)
        z = rest - (c0_re * w0 + c0_im * tw0) - (c1_re * w1 + c1_im * tw1)
    return z


def split(x):
    hi = x.astype(BF16)
    return hi, (x - hi.astype(F32)).astype(BF16)


def solve_kernel(recv, refs, out, flat, chans, result, sems):
    sources = recv.shape[0]
    ranks = refs.shape[0] * REFS
    flat[...] = recv[...].astype(F32).reshape(flat.shape)
    for h in range(2):
        for c in range(CH):
            chans[h, pl.ds(c, sources, stride=CH), :] = flat[
                pl.ds(h * CH + c, sources, stride=BINS), :
            ]

    lane = lax.broadcasted_iota(jnp.int32, (LANES, LANES), 1)
    row = lax.broadcasted_iota(jnp.int32, (LANES, LANES), 0)
    same = (lane // 32) == (row // 32)
    lane32, row32 = lane[:32], row[:32]
    inner32 = lax.rem(lane32, 32)
    ones = jnp.concatenate([jnp.where(same, 1.0, 0.0).astype(BF16)] * 3, axis=0)
    blocks, grams = [], []
    for h in range(2):
        x = refs[:, h].reshape(ranks, LANES).astype(F32)
        imag = lax.rem(lax.broadcasted_iota(jnp.int32, x.shape, 1), 32) >= SEGS
        block = jnp.concatenate([x, turn(x, imag)], axis=0).astype(BF16)
        blocks.append(block)
        gram = jnp.where(same, tn_dot(block, block), 0.0)
        gram = gram[0:32] + gram[32:64] + gram[64:96] + gram[96:128]
        diagonal = jnp.where(inner32 == row32, gram, 0.0)
        diagonal = jnp.sum(diagonal, axis=0, keepdims=True)
        hi, lo = split(diagonal)
        lost = (diagonal - hi.astype(F32) - lo.astype(F32)).astype(BF16)
        parts = jnp.concatenate([hi, lo, lost], axis=1)
        parts = jnp.broadcast_to(parts.astype(F32), (16, 3 * LANES)).astype(BF16)
        trace = jnp.dot(parts, ones, preferred_element_type=F32)
        ridge = (RIDGE / (2 * ranks)) * trace[:1]
        grams.append(gram[:SEGS] + jnp.where(inner32[:SEGS] == row32[:SEGS], ridge, 0.0))

    inverses = invert(jnp.concatenate(grams, axis=0), lane32, row32)
    imag16 = lax.rem(lane[:SEGS], 32) >= SEGS
    copies = []
    for h in range(2):
        upper = inverses[h * SEGS : (h + 1) * SEGS]
        full = jnp.concatenate([upper, turn(upper, imag16)], axis=0)
        full = jnp.where(same, jnp.concatenate([full] * 4, axis=0), 0.0)
        hi, lo = split(full)
        solved = nt_dot(hi, blocks[h]) + nt_dot(lo, blocks[h])
        y = chans[h].astype(BF16)
        y = jnp.concatenate([y, y], axis=1)
        owner = lax.broadcasted_iota(jnp.int32, solved.shape, 0) // 32
        for b in range(4):
            hi, lo = split(jnp.where(owner == b, solved, 0.0))
            weights = jnp.concatenate([hi, lo], axis=0)
            f = h * 4 + b
            result[f] = jnp.dot(y, weights, preferred_element_type=F32).astype(BF16)
            copy = pltpu.make_async_copy(result.at[f], out.at[f], sems.at[f])
            copy.start()
            copies.append(copy)
    for copy in copies:
        copy.wait()


def in_hbm(x):
    return pltpu.with_memory_space_constraint(x, pltpu.HBM)


def exchange(record, ref_index, offsets, table):
    bins, grps = lax.axis_size("bin"), lax.axis_size("grp")
    vmem = pl.BlockSpec(memory_space=pltpu.VMEM)
    hbm = pl.BlockSpec(memory_space=pltpu.HBM)
    return pl.pallas_call(
        exchange_kernel,
        out_shape=(
            jax.ShapeDtypeStruct((bins, BINS, LANES), BF16),
            jax.ShapeDtypeStruct((grps, 2, REFS, LANES), BF16),
        ),
        in_specs=[hbm, hbm, hbm, hbm],
        out_specs=(vmem, vmem),
        scratch_shapes=[
            pltpu.SMEM(offsets.shape, jnp.int32),
            pltpu.SMEM(ref_index.shape, jnp.int32),
            pltpu.VMEM(record.shape, BF16),
            pltpu.VMEM(table.shape, BF16),
            pltpu.VMEM((CH * 72, LANES), F32),
            pltpu.VMEM((2 * CH * bins, LANES), F32),
            pltpu.VMEM((bins, BINS, LANES), BF16),
            pltpu.SemaphoreType.DMA((7,)),
            pltpu.SemaphoreType.DMA((8,)),
            pltpu.SemaphoreType.REGULAR((bins,)),
            pltpu.SemaphoreType.REGULAR((grps,)),
        ],
        compiler_params=pltpu.CompilerParams(
            collective_id=0, has_side_effects=True, vmem_limit_bytes=VMEM_LIMIT
        ),
    )(*(in_hbm(x) for x in (offsets, ref_index, record, table)))


def solve(recv, refs):
    sources = recv.shape[0]
    chans = sources * CH
    vmem = pl.BlockSpec(memory_space=pltpu.VMEM)
    width = 2 * refs.shape[0] * REFS
    return pl.pallas_call(
        solve_kernel,
        out_shape=jax.ShapeDtypeStruct((BINS, chans, width), BF16),
        in_specs=[vmem, vmem],
        out_specs=pl.BlockSpec(memory_space=pl.ANY),
        scratch_shapes=[
            pltpu.VMEM((sources * BINS, LANES), F32),
            pltpu.VMEM((2, chans, LANES), F32),
            pltpu.VMEM((BINS, chans, width), BF16),
            pltpu.SemaphoreType.DMA((BINS,)),
        ],
        compiler_params=pltpu.CompilerParams(vmem_limit_bytes=VMEM_LIMIT),
    )(recv, refs)


def local(record, ref_index, offsets):
    table = jnp.asarray(make_table(lax.axis_size("bin")))
    recv, refs = exchange(record, ref_index, offsets, table)
    return solve(recv, refs)


def solution(mesh):
    placed = (P("grp", "bin", None), P("grp", None), P())
    return jax.shard_map(
        local, mesh=mesh, in_specs=placed, out_specs=P("bin", "grp", None), check_vma=False
    )
```

```python
import math

import jax
import jax.numpy as jnp
import ml_dtypes
import numpy as np
from jax import lax
from jax.experimental import pallas as pl
from jax.experimental.pallas import tpu as pltpu
from jax.sharding import PartitionSpec as P

L = 1024
NB = 512
SEGS = 16
CH = 4
BINS = 8
REFS = 16
LANES = 128
TILES = 8704 // LANES
STEPS = L // LANES + 1
RIDGE = 0.5
VMEM_LIMIT = 16 << 20

F32 = jnp.float32
BF16 = jnp.bfloat16
MESH = pl.DeviceIdType.MESH


def make_table(bin_devices):
    n = np.arange(L)
    angles = (n[:, None] * np.arange(NB)[None, :] % L).astype(np.float32)
    angles = angles * np.float32(2.0 * math.pi / L)
    hann = np.float32(0.5) - np.float32(0.5) * np.cos(
        n.astype(np.float32) * np.float32(2.0 * math.pi / L)
    )
    parts = np.stack([hann[:, None] * np.cos(angles), -(hann[:, None] * np.sin(angles))])
    parts = parts.reshape(2, L, bin_devices, 2, 4)
    return parts.transpose(4, 0, 2, 3, 1).reshape(8, LANES, L).astype(ml_dtypes.bfloat16)


def nt_dot(a, b):
    return lax.dot_general(a, b, (((1,), (1,)), ((), ())), preferred_element_type=F32)


def tn_dot(a, b):
    return lax.dot_general(a, b, (((0,), (0,)), ((), ())), preferred_element_type=F32)


def lane_pick(x, index):
    return jnp.take_along_axis(x, index, axis=1, mode="promise_in_bounds")


def cut_segments(offsets, record, tiles):
    span = tiles.shape[0] // CH
    for t in range(span):
        column = jnp.zeros((CH, LANES), F32)
        if t < TILES:
            column = record[0, :, t * LANES : (t + 1) * LANES].astype(F32)
        tiles[pl.ds(t, CH, stride=span), :] = column
    source = [tiles[pl.ds(c * span, span), :] for c in range(CH)]
    source = jnp.concatenate(source, axis=1).astype(BF16)

    row = lax.broadcasted_iota(jnp.int32, (SEGS, LANES), 0)
    lane = lax.broadcasted_iota(jnp.int32, (SEGS, LANES), 1)
    start = jnp.zeros((SEGS, LANES), jnp.int32)
    for s in range(SEGS):
        start = jnp.where(row == s, offsets[s], start)
    first = jnp.minimum(start >> 7, TILES - STEPS)
    shift = start - first * LANES
    chosen = jnp.concatenate([(first + t == lane)[:, :span] for t in range(STEPS)], axis=0)
    chosen = jnp.where(chosen, 1.0, 0.0).astype(BF16)
    window = jnp.dot(chosen, source, preferred_element_type=F32)
    window = window.reshape(STEPS, SEGS, CH * LANES)
    index = (lane + shift) & (LANES - 1)
    here = lane + shift < LANES
    rows = []
    for c in range(CH):
        turned = [
            lane_pick(window[t, :, c * LANES : (c + 1) * LANES], index) for t in range(STEPS)
        ]
        cut = [jnp.where(here, turned[t], turned[t + 1]) for t in range(STEPS - 1)]
        rows.append(jnp.concatenate(cut, axis=1))
    return jnp.concatenate(rows, axis=0).astype(BF16)


def pack_spectra(rows, table, loads, stage, send):
    rows = jnp.concatenate([rows, rows], axis=0)
    blocks = []
    for g in range(8):
        loads[g].wait()
        blocks.append(nt_dot(table[g], rows))
    group = lax.broadcasted_iota(jnp.int32, (LANES, LANES), 1) // SEGS
    turned = []
    for r in range(4):
        mixed = blocks[r]
        for q in range(1, 8):
            mixed = jnp.where(group == q, blocks[(q + r) % 8], mixed)
        turned.append(pltpu.roll(mixed, SEGS * r, axis=1) if r else mixed)
    phase = lax.rem(group, 4)
    for c in range(CH):
        out = turned[(0 - c) % 4]
        for g in range(1, 4):
            out = jnp.where(phase == g, turned[(g - c) % 4], out)
        stage[pl.ds(c, LANES, stride=CH), :] = out
    send[...] = stage[...].reshape(send.shape).astype(BF16)


def pick_references(ref_index, recv):
    shape = (2 * REFS, recv.shape[0] * BINS)
    row = lax.broadcasted_iota(jnp.int32, shape, 0)
    col = lax.broadcasted_iota(jnp.int32, shape, 1)
    wanted = jnp.full((2 * REFS, 1), -1, jnp.int32)
    slot = lax.broadcasted_iota(jnp.int32, (2 * REFS, 1), 0)
    for i in range(REFS):
        wanted = jnp.where(lax.rem(slot, REFS) == i, ref_index[0, i], wanted)
    place = (wanted // CH) * BINS + lax.rem(wanted, CH) + (row // REFS) * CH
    chosen = jnp.where(col == place, 1.0, 0.0).astype(BF16)
    rows = recv[...].astype(F32).reshape(shape[1], LANES).astype(BF16)
    return jnp.dot(chosen, rows, preferred_element_type=F32).astype(BF16)


def exchange_kernel(
    offsets_hbm,
    ref_index_hbm,
    record_hbm,
    table_hbm,
    recv,
    refs,
    offsets,
    ref_index,
    record,
    table,
    tiles,
    stage,
    send,
    sems,
    table_sems,
    bin_in,
    grp_in,
):
    bins, grps = lax.axis_size("bin"), lax.axis_size("grp")
    me, grp = lax.axis_index("bin"), lax.axis_index("grp")
    grp_rank = grp + lax.rem(me, 2) * (grps - 1 - 2 * grp)

    def in_grp(k):
        return {"grp": k + lax.rem(me, 2) * (grps - 1 - 2 * k)}

    load_offsets = pltpu.make_async_copy(offsets_hbm, offsets, sems.at[0])
    load_record = pltpu.make_async_copy(record_hbm, record, sems.at[5])
    load_refs = pltpu.make_async_copy(ref_index_hbm, ref_index, sems.at[6])
    loads = [
        pltpu.make_async_copy(table_hbm.at[g], table.at[g], table_sems.at[g]) for g in range(8)
    ]
    for load in (load_record, load_offsets, *loads, load_refs):
        load.start()

    barrier = pltpu.get_barrier_semaphore()

    @pl.loop(0, bins - 1 - me)
    def _(k):
        peer = bins - 1 - k
        pl.semaphore_signal(barrier, 1, device_id={"bin": peer}, device_id_type=MESH)

    @pl.loop(grp_rank + 1, grps)
    def _(k):
        pl.semaphore_signal(barrier, 1, device_id=in_grp(k), device_id_type=MESH)

    load_offsets.wait()
    load_record.wait()
    rows = cut_segments(offsets, record, tiles)
    pack_spectra(rows, table, loads, stage, send)

    before = me + grp_rank

    @pl.when(before > 0)
    def _():
        pl.semaphore_wait(barrier, before)

    def send_to(peer):
        pltpu.make_async_remote_copy(
            src_ref=send.at[peer],
            dst_ref=recv.at[me],
            send_sem=sems.at[1],
            recv_sem=sems.at[2],
            device_id={"bin": peer},
            device_id_type=MESH,
        ).start()

    @pl.loop(0, me)
    def _(peer):
        send_to(peer)
        pl.semaphore_signal(bin_in.at[me], 1, device_id={"bin": peer}, device_id_type=MESH)

    @pl.loop(0, grp_rank)
    def _(k):
        pl.semaphore_signal(grp_in.at[grp_rank], 1, device_id=in_grp(k), device_id_type=MESH)

    recv[pl.ds(me, 1)] = send[pl.ds(me, 1)]

    @pl.loop(me + 1, bins)
    def _(peer):
        pl.semaphore_wait(bin_in.at[peer], 1)
        send_to(peer)

    @pl.loop(grp_rank + 1, grps)
    def _(k):
        pl.semaphore_wait(grp_in.at[k], 1)

    load_refs.wait()
    others = recv.at[pl.ds(0, bins - 1)]
    pltpu.make_async_copy(others, others, sems.at[2]).wait()
    refs[pl.ds(grp, 1)] = pick_references(ref_index, recv).reshape(1, 2, REFS, LANES)

    upper = grp // (grps // 2)

    @pl.loop(0, grps)
    def _(k):
        peer = upper * k + (1 - upper) * (grps - 1 - k)

        @pl.when(peer != grp)
        def _():
            pltpu.make_async_remote_copy(
                src_ref=refs.at[grp],
                dst_ref=refs.at[grp],
                send_sem=sems.at[3],
                recv_sem=sems.at[4],
                device_id={"grp": peer},
                device_id_type=MESH,
            ).start()

    sent = send.at[pl.ds(0, bins - 1)]
    pltpu.make_async_copy(sent, sent, sems.at[1]).wait()
    other_refs = refs.at[pl.ds(0, grps - 1)]
    pltpu.make_async_copy(other_refs, other_refs, sems.at[4]).wait()
    pltpu.make_async_copy(other_refs, other_refs, sems.at[3]).wait()


def turn(x, imag):
    back = pltpu.roll(x, LANES - SEGS, axis=1)
    ahead = pltpu.roll(x, SEGS, axis=1)
    return jnp.where(imag, ahead, -back)


def invert(z, lane, row):
    inner = lax.rem(lane, 32)
    base = lane - inner
    column = lax.rem(lane, SEGS)
    segment = lax.rem(row, SEGS)
    few = slice(0, 2)
    imag, base2 = inner[few] >= SEGS, base[few]

    def pivot_row(k):
        return jnp.concatenate([z[k : k + 1], z[SEGS + k : SEGS + k + 1]], axis=0)

    def spread(x):
        return jnp.concatenate(
            [jnp.broadcast_to(x[h : h + 1], (SEGS, LANES)) for h in range(2)], axis=0
        )

    for k in range(0, SEGS, 2):
        m = k + 1
        in_cols = (column == k) | (column == m)
        r0, r1 = pivot_row(k), pivot_row(m)
        a = lane_pick(r0, base2 + k)
        b_re = lane_pick(r0, base2 + m)
        b_im = lane_pick(r0, base2 + (SEGS + m))
        d = lane_pick(r1, base2 + m)
        inverse = 1.0 / (a * d - (b_re * b_re + b_im * b_im))
        a, d, b_re, b_im = a * inverse, d * inverse, b_re * inverse, b_im * inverse
        e0 = jnp.where(in_cols[few], jnp.where(inner[few] == k, 1.0, 0.0), r0)
        e1 = jnp.where(in_cols[few], jnp.where(inner[few] == m, 1.0, 0.0), r1)
        t0, t1 = turn(e0, imag), turn(e1, imag)
        w0 = spread(d * e0 - b_re * e1 - b_im * t1)
        w1 = spread(a * e1 - b_re * e0 + b_im * t0)
        tw0 = spread(d * t0 - b_re * t1 + b_im * e1)
        tw1 = spread(a * t1 - b_re * t0 - b_im * e0)
        is0, is1 = segment == k, segment == m
        is_row = is0 | is1
        c0_re = jnp.where(is_row, jnp.where(is0, -1.0, 0.0), lane_pick(z, base + k))
        c0_im = jnp.where(is_row, 0.0, lane_pick(z, base + (SEGS + k)))
        c1_re = jnp.where(is_row, jnp.where(is1, -1.0, 0.0), lane_pick(z, base + m))
        c1_im = jnp.where(is_row, 0.0, lane_pick(z, base + (SEGS + m)))
        rest = jnp.where(is_row | in_cols, 0.0, z)
        z = rest - (c0_re * w0 + c0_im * tw0) - (c1_re * w1 + c1_im * tw1)
    return z


def split(x):
    hi = x.astype(BF16)
    return hi, (x - hi.astype(F32)).astype(BF16)


def solve_kernel(recv, refs, out, flat, chans, result, sems):
    sources = recv.shape[0]
    ranks = refs.shape[0] * REFS
    flat[...] = recv[...].astype(F32).reshape(flat.shape)
    for h in range(2):
        for c in range(CH):
            chans[h, pl.ds(c, sources, stride=CH), :] = flat[
                pl.ds(h * CH + c, sources, stride=BINS), :
            ]

    lane = lax.broadcasted_iota(jnp.int32, (LANES, LANES), 1)
    row = lax.broadcasted_iota(jnp.int32, (LANES, LANES), 0)
    same = (lane // 32) == (row // 32)
    lane32, row32 = lane[:32], row[:32]
    inner32 = lax.rem(lane32, 32)
    blocks, grams, ridges = [], [], []
    for h in range(2):
        x = refs[:, h].reshape(ranks, LANES).astype(F32)
        imag = lax.rem(lax.broadcasted_iota(jnp.int32, x.shape, 1), 32) >= SEGS
        block = jnp.concatenate([x, turn(x, imag)], axis=0).astype(BF16)
        blocks.append(block)
        gram = jnp.where(same, tn_dot(block, block), 0.0)
        gram = gram[0:32] + gram[32:64] + gram[64:96] + gram[96:128]
        diagonal = jnp.where(inner32 == row32, gram, 0.0)
        diagonal = jnp.sum(diagonal, axis=0, keepdims=True)
        group_ones = jnp.where(same, 1.0, 0.0)
        trace = jnp.dot(
            jnp.broadcast_to(diagonal, (8, LANES)),
            group_ones,
            precision=lax.Precision.HIGHEST,
            preferred_element_type=F32,
        )
        ridge = (RIDGE / (2 * ranks)) * trace[:1]
        grams.append(gram[:SEGS] + jnp.where(inner32[:SEGS] == row32[:SEGS], ridge, 0.0))

    inverses = invert(jnp.concatenate(grams, axis=0), lane32, row32)
    imag16 = lax.rem(lane[:SEGS], 32) >= SEGS
    copies = []
    for h in range(2):
        upper = inverses[h * SEGS : (h + 1) * SEGS]
        full = jnp.concatenate([upper, turn(upper, imag16)], axis=0)
        full = jnp.where(same, jnp.concatenate([full] * 4, axis=0), 0.0)
        hi, lo = split(full)
        solved = nt_dot(hi, blocks[h]) + nt_dot(lo, blocks[h])
        y = chans[h].astype(BF16)
        y = jnp.concatenate([y, y], axis=1)
        owner = lax.broadcasted_iota(jnp.int32, solved.shape, 0) // 32
        for b in range(4):
            hi, lo = split(jnp.where(owner == b, solved, 0.0))
            weights = jnp.concatenate([hi, lo], axis=0)
            f = h * 4 + b
            result[f] = jnp.dot(y, weights, preferred_element_type=F32).astype(BF16)
            copy = pltpu.make_async_copy(result.at[f], out.at[f], sems.at[f])
            copy.start()
            copies.append(copy)
    for copy in copies:
        copy.wait()


def in_hbm(x):
    return pltpu.with_memory_space_constraint(x, pltpu.HBM)


def exchange(record, ref_index, offsets, table):
    bins, grps = lax.axis_size("bin"), lax.axis_size("grp")
    vmem = pl.BlockSpec(memory_space=pltpu.VMEM)
    hbm = pl.BlockSpec(memory_space=pltpu.HBM)
    return pl.pallas_call(
        exchange_kernel,
        out_shape=(
            jax.ShapeDtypeStruct((bins, BINS, LANES), BF16),
            jax.ShapeDtypeStruct((grps, 2, REFS, LANES), BF16),
        ),
        in_specs=[hbm, hbm, hbm, hbm],
        out_specs=(vmem, vmem),
        scratch_shapes=[
            pltpu.SMEM(offsets.shape, jnp.int32),
            pltpu.SMEM(ref_index.shape, jnp.int32),
            pltpu.VMEM(record.shape, BF16),
            pltpu.VMEM(table.shape, BF16),
            pltpu.VMEM((CH * 72, LANES), F32),
            pltpu.VMEM((2 * CH * bins, LANES), F32),
            pltpu.VMEM((bins, BINS, LANES), BF16),
            pltpu.SemaphoreType.DMA((7,)),
            pltpu.SemaphoreType.DMA((8,)),
            pltpu.SemaphoreType.REGULAR((bins,)),
            pltpu.SemaphoreType.REGULAR((grps,)),
        ],
        compiler_params=pltpu.CompilerParams(
            collective_id=0, has_side_effects=True, vmem_limit_bytes=VMEM_LIMIT
        ),
    )(*(in_hbm(x) for x in (offsets, ref_index, record, table)))


def solve(recv, refs):
    sources = recv.shape[0]
    chans = sources * CH
    vmem = pl.BlockSpec(memory_space=pltpu.VMEM)
    width = 2 * refs.shape[0] * REFS
    return pl.pallas_call(
        solve_kernel,
        out_shape=jax.ShapeDtypeStruct((BINS, chans, width), BF16),
        in_specs=[vmem, vmem],
        out_specs=pl.BlockSpec(memory_space=pl.ANY),
        scratch_shapes=[
            pltpu.VMEM((sources * BINS, LANES), F32),
            pltpu.VMEM((2, chans, LANES), F32),
            pltpu.VMEM((BINS, chans, width), BF16),
            pltpu.SemaphoreType.DMA((BINS,)),
        ],
        compiler_params=pltpu.CompilerParams(vmem_limit_bytes=VMEM_LIMIT),
    )(recv, refs)


def local(record, ref_index, offsets):
    table = jnp.asarray(make_table(lax.axis_size("bin")))
    recv, refs = exchange(record, ref_index, offsets, table)
    return solve(recv, refs)


def solution(mesh):
    placed = (P("grp", "bin", None), P("grp", None), P())
    return jax.shard_map(
        local, mesh=mesh, in_specs=placed, out_specs=P("bin", "grp", None), check_vma=False
    )
```
